32 devices in a mesh: seq: 16 (over z, y, core), head: 2 (over x).
Axes of the slice: x: 2, y: 2, z: 4, core: 2. Of those that a mesh axis runs over, the one named last changes fastest.
Arguments:
- inputs: bfloat16 [16384, 4096], P('seq', 'head'), may hold values from -0.625 to 0.625
- grad_out: bfloat16 [16384, 4096], P('seq', 'head'), may hold values from -0.3125 to 0.3125
- b_proj: bfloat16 [16384, 128], P('seq'), may hold values from -0.5 to 0.5
- c_proj: bfloat16 [16384, 128], P('seq'), may hold values from -0.5 to 0.5
- log_forgetting: float32 [64, 16384], P('head', 'seq'), may hold values from -0.9 to 0, as said below
- bounds: int32 [4], replicated, may hold values from 1 to 8191, as said below
Outputs:
- grad_inputs: bfloat16 [16384, 4096], P('seq', 'head')
- grad_b: bfloat16 [16384, 128], P(('seq', 'head'))
- grad_c: bfloat16 [16384, 128], P(('seq', 'head'))
- grad_log_decay: float32 [64, 16384], P('head', 'seq')
The draws below stay inside these ranges and needn't reach their ends.
Inputs may be any that keep to these rules, and one draw needn't show every extreme that they name: `bounds`: 4 distinct indices in increasing order. `log_forgetting`: negative values.
All inputs are finite; a program needn't handle non-finite values.
Results may differ from the reference program's by a relative error of at most 0.001.
Values sent between devices are 32-bit elements; how exact they have to be, the bound alone decides.
No kernel may reach another device: no remote copies, remote signals or barrier semaphores. Data moves between devices by JAX's collectives and lax.ppermute only.
A program may use at most 192 MiB of HBM per device.

```python
import math
import jax
import jax.numpy as jnp
from jax import lax

H = 64
P_SIZE = 64
N = 128
BLOCK = 256
BOUNDS = 4
TOTAL_TOKENS = 16384


def draw_log_forgetting(key, part):
    stochastic_seeds = jax.random.split(key, 7)
    fast_share = 0.5
    is_fast = jax.random.uniform(stochastic_seeds[0], (H, 1)) < fast_share
    fast_rate = jnp.exp(jax.random.uniform(stochastic_seeds[1], (H, 1), jnp.float32, math.log(0.02), math.log(0.035)))
    slow_rate = jnp.exp(jax.random.uniform(stochastic_seeds[2], (H, 1), jnp.float32, math.log(0.1), math.log(1.0))) / TOTAL_TOKENS
    channel_forgetting_speed = jnp.where(is_fast, fast_rate, slow_rate)
    trial_extent_factor = jnp.exp(jax.random.uniform(stochastic_seeds[3], (H, TOTAL_TOKENS // BLOCK), jnp.float32, math.log(0.5), math.log(2.0)))
    trial_extent_factor = jnp.repeat(trial_extent_factor, BLOCK, axis=1)
    stochastic_shift = jax.random.uniform(stochastic_seeds[4], (H, TOTAL_TOKENS), jnp.float32, 0.5, 2.0)
    present_stretch = jax.random.uniform(stochastic_seeds[5], (1, TOTAL_TOKENS)) < 3.0 / TOTAL_TOKENS
    stretch_count = -jnp.log(jax.random.uniform(stochastic_seeds[6], (1, TOTAL_TOKENS), jnp.float32, 0.5, 0.8))
    log_forgetting = -(channel_forgetting_speed * trial_extent_factor * stochastic_shift) - jnp.where(present_stretch, stretch_count, 0.0)
    return log_forgetting.astype(jnp.float32)


def draw_bounds(key, part):
    half_len = TOTAL_TOKENS // 2
    picked = jax.random.permutation(key, half_len - 2)[:BOUNDS - 1] + 1
    last_one = jnp.full((1,), half_len - 1, jnp.int32)
    joined = jnp.concatenate([picked.astype(jnp.int32), last_one], axis=0)
    return jnp.sort(joined).astype(jnp.int32)


def block_levels(rng, dims, cuts, smallest, top_value):
    def one(dim, shards_of):
        draws = jax.random.uniform(jax.random.fold_in(jax.random.fold_in(rng, 6), dim), (shards_of,), jnp.float32, smallest / len(cuts), top_value / len(cuts))
        return jnp.repeat(jnp.exp(draws), dims[dim] // shards_of).reshape((-1,) + (1,) * (len(dims) - dim - 1))

    gain = one(*cuts[0])
    for cut in cuts[1:]:
        gain = gain * one(*cut)
    return gain


def bell_draw(rng, shape, width, reach, cuts=(), held_as=jnp.bfloat16):
    values = jax.random.normal(rng, shape, jnp.float32) * width
    if len(cuts) > 0:
        values = block_levels(rng, shape, cuts, -0.22, 0.18) * values
    return jnp.clip(values, min=-reach, max=reach).astype(held_as)


def setup_inputs(seed: int = 0) -> dict:
    key_list = jax.random.split(jax.random.key(seed), 7)
    inputs = bell_draw(key_list[0], (TOTAL_TOKENS, H * P_SIZE), 0.1, 0.625, ((0, 16), (1, 2)))
    grad_out = bell_draw(key_list[1], (TOTAL_TOKENS, H * P_SIZE), 0.05, 0.3125, ((0, 16), (1, 2)))
    b_proj = bell_draw(key_list[2], (TOTAL_TOKENS, N), 0.09, 0.5, ((0, 16),))
    c_proj = bell_draw(key_list[3], (TOTAL_TOKENS, N), 0.09, 0.5, ((0, 16),))
    log_forgetting = draw_log_forgetting(jax.random.fold_in(key_list[6], 71), 0)
    bounds = draw_bounds(jax.random.fold_in(key_list[6], 71), 0)
    return {"inputs": inputs, "grad_out": grad_out, "b_proj": b_proj, "c_proj": c_proj, "log_forgetting": log_forgetting, "bounds": bounds}


def chain_prefix(totals, sums, reverse):
    def advance(running, pieces):
        acc_total, acc_sum = running
        blk_total, blk_sum = pieces
        return (acc_total * blk_total, blk_total[:, None, None] * acc_sum + blk_sum), (acc_total, acc_sum)

    start = (jnp.ones(totals.shape[1:], jnp.float32), jnp.zeros(sums.shape[1:], jnp.float32))
    return lax.scan(advance, start, (totals, sums), reverse=reverse)


def block_grads(pieces):
    x_blk, dy_blk, b_blk, c_blk, cumulative, segments, from_start, to_end, state_in, costate_in, totals = pieces
    highest = lax.Precision.HIGHEST
    block_len = cumulative.shape[-1]
    row_ids = lax.broadcasted_iota(jnp.int32, (block_len, block_len), 0)
    col_ids = lax.broadcasted_iota(jnp.int32, (block_len, block_len), 1)
    lower_tri = row_ids >= col_ids
    linked = lower_tri & (segments[:, None] == segments[None, :])
    log_gap = jnp.where(lower_tri[None], cumulative[:, :, None] - cumulative[:, None, :], 0.0)
    decays = jnp.where(linked[None], jnp.exp(log_gap), 0.0)
    x_wide = x_blk.astype(jnp.float32)
    dy_wide = dy_blk.astype(jnp.float32)
    b_wide = b_blk.astype(jnp.float32)
    c_wide = c_blk.astype(jnp.float32)
    intersections = jnp.einsum('tn,sn->ts', c_wide, b_wide, precision=highest)
    products = jnp.einsum('thp,shp->hts', dy_wide, x_wide, precision=highest)
    scored = decays * intersections[None]
    mixture = scored * products
    weights = jnp.sum(decays * products, axis=0)
    end_share = jnp.transpose(to_end)[:, :, None]
    start_share = jnp.transpose(from_start)[:, :, None]
    dx_local = jnp.einsum('hts,thp->shp', scored, dy_wide, precision=highest)
    carried = jnp.einsum('sn,hnp->shp', b_wide, costate_in, precision=highest)
    grad_x = (dx_local + end_share * carried).astype(jnp.bfloat16)
    grad_b = jnp.dot(jnp.transpose(weights), c_wide, precision=highest) + jnp.einsum('hnp,shp->sn', costate_in, x_wide * end_share, precision=highest)
    grad_c = jnp.dot(weights, b_wide, precision=highest) + jnp.einsum('hnp,thp->tn', state_in, dy_wide * start_share, precision=highest)
    balance = jnp.sum(mixture, axis=1) - jnp.sum(mixture, axis=2)
    inside = jnp.cumsum(balance, axis=1) - balance
    read_out = jnp.einsum('tn,hnp->thp', c_wide, state_in, precision=highest)
    later_terms = jnp.transpose(jnp.sum(read_out * dy_wide, axis=2)) * from_start
    suffix = jnp.flip(jnp.cumsum(jnp.flip(later_terms, 1), axis=1), 1)
    early_terms = jnp.transpose(jnp.sum(carried * x_wide, axis=2)) * to_end
    prefix = jnp.cumsum(early_terms, axis=1) - early_terms
    joined = totals * jnp.sum(costate_in * state_in, axis=(1, 2))
    grad_log = inside + suffix + prefix + joined[:, None]
    return grad_x, grad_b, grad_c, grad_log


def reference(inputs, grad_out, b_proj, c_proj, log_forgetting, bounds):
    highest = lax.Precision.HIGHEST
    tokens = inputs.shape[0]
    n_blocks = tokens // BLOCK
    positions = lax.broadcasted_iota(jnp.int32, (tokens, BOUNDS), 0)
    resets = jnp.sum(jnp.where(positions == bounds[None, :].astype(jnp.int32), 1.0, 0.0), axis=1).astype(jnp.float32)
    segments = jnp.cumsum(resets.reshape(n_blocks, BLOCK), axis=1)
    rates = jnp.transpose(log_forgetting.reshape(H, n_blocks, BLOCK), (1, 0, 2))
    cumulative = jnp.cumsum(rates, axis=2)
    from_start = jnp.exp(cumulative) * jnp.where(segments == 0.0, 1.0, 0.0)[:, None, :]
    to_end = jnp.exp(cumulative[:, :, -1:] - cumulative) * jnp.where(segments[:, -1:] == segments, 1.0, 0.0)[:, None, :]
    totals = from_start[:, :, -1]
    x_blocks = inputs.reshape(n_blocks, BLOCK, H, P_SIZE)
    dy_blocks = grad_out.reshape(n_blocks, BLOCK, H, P_SIZE)
    b_blocks = b_proj.reshape(n_blocks, BLOCK, N)
    c_blocks = c_proj.reshape(n_blocks, BLOCK, N)

    def summaries(pieces):
        x_blk, dy_blk, b_blk, c_blk, start_w, end_w = pieces
        state_part = jnp.einsum('qn,qhp->hnp', b_blk.astype(jnp.float32), x_blk.astype(jnp.float32) * jnp.transpose(end_w)[:, :, None], precision=highest)
        costate_part = jnp.einsum('qn,qhp->hnp', c_blk.astype(jnp.float32), dy_blk.astype(jnp.float32) * jnp.transpose(start_w)[:, :, None], precision=highest)
        return state_part, costate_part

    state_parts, costate_parts = lax.map(summaries, (x_blocks, dy_blocks, b_blocks, c_blocks, from_start, to_end))
    whole_fwd, before_fwd = chain_prefix(totals, state_parts, False)
    whole_bwd, before_bwd = chain_prefix(totals, costate_parts, True)
    results = lax.map(block_grads, (x_blocks, dy_blocks, b_blocks, c_blocks, cumulative, segments, from_start, to_end, before_fwd[1], before_bwd[1], totals))
    grad_inputs = results[0].reshape(tokens, H * P_SIZE)
    grad_b = results[1].reshape(tokens, N).astype(jnp.bfloat16)
    grad_c = results[2].reshape(tokens, N).astype(jnp.bfloat16)
    grad_log_decay = jnp.transpose(results[3], (1, 0, 2)).reshape(H, tokens)
    return grad_inputs, grad_b, grad_c, grad_log_decay
```

```python
import functools

import jax
import jax.numpy as jnp
from jax import lax
from jax.experimental import pallas as pl
from jax.experimental.pallas import tpu as pltpu
from jax.sharding import PartitionSpec as P

P_SIZE = 64
N = 128
BLOCK = 256
TILE = 256
HPT = TILE // P_SIZE
LANES = 128
OUTER = 4
LOG2E = 1.4426950408889634
F32 = jnp.float32
BF16 = jnp.bfloat16

NN = (((1,), (0,)), ((), ()))
NT = (((1,), (1,)), ((), ()))
TN = (((0,), (0,)), ((), ()))


def mm(a, b, dims=NN):
    return lax.dot_general(a, b, dims, preferred_element_type=F32)


def split2(v):
    hi = v.astype(BF16)
    return hi, (v - hi.astype(F32)).astype(BF16)


def split3(v):
    hi = v.astype(BF16)
    rest = v - hi.astype(F32)
    mid = rest.astype(BF16)
    return hi, mid, (rest - mid.astype(F32)).astype(BF16)


def iota2(shape, dim):
    return lax.broadcasted_iota(jnp.int32, shape, dim)


def ones_where(cond):
    return jnp.where(cond, 1.0, 0.0).astype(BF16)


def expander(first_head, parts, width_bits, cols):
    r = iota2((parts * LANES, cols), 0) & (LANES - 1)
    c = iota2((parts * LANES, cols), 1) >> width_bits
    return ones_where(r == c + first_head)


def collector(first_head, cols):
    c = iota2((cols, LANES), 0) >> 6
    h = iota2((cols, LANES), 1)
    return ones_where(h == c + first_head)


def expand(v, onehot2):
    hi, lo = split2(v)
    return mm(jnp.concatenate([hi, lo], axis=1), onehot2)


def collect(v, onehot):
    hi, lo = split2(v)
    return mm(hi, onehot) + mm(lo, onehot)


def tri(cond_of):
    return ones_where(cond_of(iota2((BLOCK, BLOCK), 0), iota2((BLOCK, BLOCK), 1)))


def prep_kernel(nb, nbounds, bounds, off, lf_ref, cumt_ref, cumr_ref, fsb_ref, teb_ref, fsd_ref, ted_ref):
    hl = lf_ref.shape[0]
    tok = nb * BLOCK
    lower = tri(lambda t, s: s <= t)
    upper = tri(lambda s, t: s <= t)
    run = jnp.zeros((1, LANES), F32)
    starts = []
    for b in range(nb):
        rows = slice(b * BLOCK, (b + 1) * BLOCK)
        lf = lf_ref[:, rows]
        lf_pad = jnp.concatenate([lf, jnp.zeros((LANES - hl, BLOCK), F32)], axis=0)
        parts = split3(lf_pad)
        cumt = sum(mm(lower, p, NT) for p in parts)
        cumr = sum(mm(p, upper) for p in parts)
        cumt_ref[rows, :] = cumt * LOG2E
        cumr_ref[:, rows] = cumr[:hl] * LOG2E
        starts.append(run)
        run = run + cumt[BLOCK - 1 : BLOCK]
    total = run
    t_loc = iota2((BLOCK, LANES), 0)
    for b in range(nb):
        rows = slice(b * BLOCK, (b + 1) * BLOCK)
        cumt = cumt_ref[rows, :] * (1.0 / LOG2E)
        last = cumt[BLOCK - 1 : BLOCK]
        t = t_loc + b * BLOCK
        cut_fb = jnp.zeros((BLOCK, LANES), jnp.bool_)
        cut_tb = cut_fb
        cut_fd = cut_fb
        cut_td = cut_fb
        for k in range(nbounds):
            bk = bounds[k] - off[0]
            cut_fd = cut_fd | ((bk >= 0) & (bk <= t))
            cut_td = cut_td | ((bk < tok) & (bk > t))
            cut_fb = cut_fb | ((bk >= b * BLOCK) & (bk <= t))
            cut_tb = cut_tb | ((bk < (b + 1) * BLOCK) & (bk > t))
        dev = starts[b] + cumt
        fsb_ref[rows, :] = jnp.where(cut_fb, 0.0, jnp.exp(cumt))
        teb_ref[rows, :] = jnp.where(cut_tb, 0.0, jnp.exp(jnp.minimum(last - cumt, 0.0)))
        fsd_ref[rows, :] = jnp.where(cut_fd, 0.0, jnp.exp(dev))
        ted_ref[rows, :] = jnp.where(cut_td, 0.0, jnp.exp(jnp.minimum(total - dev, 0.0)))


def stack2(v):
    hi, lo = split2(v)
    return jnp.concatenate([hi, lo], axis=0)


def summary_kernel(nb, head0, x_ref, dy_ref, b_ref, c_ref, fsb_ref, teb_ref, pay_ref, sst_ref, gst_ref, j_ref):
    first = head0 + pl.program_id(0) * HPT
    oh2 = expander(first, 2, 6, TILE)
    state = jnp.zeros((N, TILE), F32)
    states = []
    tots = []
    for b in range(nb):
        rows = slice(b * BLOCK, (b + 1) * BLOCK)
        states.append(state)
        sst_ref[b] = stack2(state)
        te = expand(teb_ref[rows, :], oh2)
        tot = expand(fsb_ref[(b + 1) * BLOCK - 8 : (b + 1) * BLOCK, :], oh2)[7:8]
        tots.append(tot)
        hi, lo = split2(x_ref[rows, :].astype(F32) * te)
        bb = b_ref[rows, :]
        state = tot * state + (mm(bb, hi, TN) + mm(bb, lo, TN))
    pay_ref[0:N] = state
    costate = jnp.zeros((N, TILE), F32)
    whole = jnp.ones((1, TILE), F32)
    for b in reversed(range(nb)):
        rows = slice(b * BLOCK, (b + 1) * BLOCK)
        gst_ref[b] = stack2(costate)
        j_ref[b : b + 1, :] = tots[b] * jnp.sum(states[b] * costate, axis=0, keepdims=True)
        fs = expand(fsb_ref[rows, :], oh2)
        hi, lo = split2(dy_ref[rows, :].astype(F32) * fs)
        cc = c_ref[rows, :]
        costate = tots[b] * costate + (mm(cc, hi, TN) + mm(cc, lo, TN))
        whole = whole * tots[b]
    pay_ref[N : 2 * N] = costate
    pay_ref[2 * N : 2 * N + 8] = jnp.broadcast_to(whole, (8, TILE))
    for b in range(nb, j_ref.shape[0]):
        j_ref[b : b + 1, :] = jnp.zeros((1, TILE), F32)


def contract_states(scaled, stacked):
    hi, lo = split2(scaled)
    both = mm(hi, stacked, NT)
    return both[:, :N] + both[:, N:] + mm(lo, stacked[:N], NT)


def local_kernel(blk, head0, tiles, nbounds, chained, acc_in, *refs):
    refs = list(refs)
    bounds, off = refs[:2]
    x_ref, dy_ref, b_ref, c_ref, cumt_ref, cumr_ref, fsb_ref, teb_ref, sst_ref, gst_ref, j_ref = refs[2:13]
    refs = refs[13:]
    if chained:
        prev_gb, prev_gc, prev_gl = refs[1:4]
        refs = refs[4:]
    dx_ref, gb_ref, gc_ref, gl_ref, gt, wt, gb, gc, later, col, rows_s, jn = refs
    j = pl.program_id(0)
    first = head0 + j * HPT
    half = BLOCK // 2

    @pl.when(j == 0)
    def _():
        s = iota2((BLOCK, BLOCK), 0)
        t = iota2((BLOCK, BLOCK), 1)
        ok = s <= t
        for k in range(nbounds):
            bk = bounds[k] - off[0] - blk * BLOCK
            ok = ok & ((s >= bk) | (t < bk))
        gt[...] = jnp.where(ok, mm(b_ref[...], c_ref[...], NT), 0.0)
        wt[...] = jnp.zeros_like(wt)
        gb[...] = prev_gb[...] if acc_in else jnp.zeros_like(gb)
        gc[...] = prev_gc[...] if acc_in else jnp.zeros_like(gc)
        later[...] = jnp.zeros_like(later)
        col[...] = jnp.zeros_like(col)
        rows_s[...] = jnp.zeros_like(rows_s)
        jn[...] = jnp.zeros_like(jn)

    oh2 = expander(first, 2, 6, TILE)
    te = expand(teb_ref[...], oh2)
    fs = expand(fsb_ref[...], oh2)
    sst = sst_ref[0]
    gst = gst_ref[0]
    bb = b_ref[...]
    cc = c_ref[...]
    carried = te * mm(jnp.concatenate([bb, bb], axis=1), gst)
    read_out = mm(jnp.concatenate([cc, cc], axis=1), sst)
    colb = mm(jnp.concatenate(split3(cumt_ref[...]), axis=1), expander(first, 3, 7, HPT * LANES))
    low_lane = iota2((BLOCK, LANES), 1) < P_SIZE
    for p in range(HPT // 2):
        lanes = slice(p * LANES, (p + 1) * LANES)
        xp = x_ref[:, lanes]
        dyp = dy_ref[:, lanes]
        top = carried[:half, lanes]
        bot = carried[half:, lanes]
        for q in range(2):
            k = 2 * p + q
            dym = jnp.where(low_lane if q == 0 else ~low_lane, dyp, jnp.zeros_like(dyp))
            p0 = mm(xp[:half], dym, NT)
            p1 = mm(xp[half:], dym[half:], NT)
            cr = cumr_ref[pl.ds(first + k, 1), :]
            cb = colb[:, k * LANES : (k + 1) * LANES]
            d00 = jnp.exp2(jnp.minimum(cr[:, :half] - cb[:half], 0.0))
            d01 = jnp.exp2(jnp.minimum(cr[:, half:] - cb[:half], 0.0))
            d11 = jnp.exp2(jnp.minimum(cr[:, half:] - cb[half:], 0.0))
            a00 = p0[:, :half] * d00
            a01 = p0[:, half:] * d01
            a11 = p1 * d11
            wt[:half, :half] += a00
            wt[:half, half:] += a01
            wt[half:, half:] += a11
            g00 = gt[:half, :half]
            g01 = gt[:half, half:]
            g11 = gt[half:, half:]
            rows_s[pl.ds(first + k, 1), :] = jnp.concatenate(
                [
                    jnp.sum(a00 * g00, axis=0, keepdims=True),
                    jnp.sum(a01 * g01 + a11 * g11, axis=0, keepdims=True),
                ],
                axis=1,
            )
            h00, l00 = split2(d00 * g00)
            h01, l01 = split2(d01 * g01)
            h11, l11 = split2(d11 * g11)
            top = top + mm(jnp.concatenate([h00, h01], axis=1), dym)
            top = top + mm(jnp.concatenate([l00, l01], axis=1), dym)
            bot = bot + mm(jnp.concatenate([h11, l11], axis=1), jnp.concatenate([dym[half:], dym[half:]], axis=0))
        dx_ref[:half, lanes] = top
        dx_ref[half:, lanes] = bot
    pick = collector(first, TILE)
    x = x_ref[...].astype(F32)
    dys = dy_ref[...].astype(F32) * fs
    col[...] += collect(x * dx_ref[...], pick)
    later[...] += collect(dys * read_out, pick)
    gc[...] += contract_states(dys, sst)
    gb[...] += contract_states(x * te, gst)
    jn[...] += collect(jnp.broadcast_to(j_ref[blk : blk + 1, :], (8, TILE)), pick)

    @pl.when(j == tiles - 1)
    def _():
        s = iota2((BLOCK, BLOCK), 0)
        t = iota2((BLOCK, BLOCK), 1)
        ok = s <= t
        for k in range(nbounds):
            bk = bounds[k] - off[0] - blk * BLOCK
            ok = ok & ((s >= bk) | (t < bk))
        hi, lo = split2(jnp.where(ok, wt[...], 0.0))
        gb_ref[...] = gb[...] + mm(hi, cc) + mm(lo, cc)
        gc_ref[...] = gc[...] + mm(hi, bb, TN) + mm(lo, bb, TN)
        before = tri(lambda a, r: r < a)
        onward = tri(lambda a, r: r >= a)
        upper = tri(lambda r, a: r < a)
        glt = sum(mm(before, v) for v in split3(col[...])) + sum(mm(onward, v) for v in split3(later[...]))
        glt = glt + jn[0:1, :]
        rows_cum = sum(mm(v, upper) for v in split3(rows_s[...]))
        gl = jnp.transpose(glt)[: rows_s.shape[0]] - rows_cum
        gl_ref[...] = gl + prev_gl[...] if acc_in else gl


def enter_kernel(nb, head0, tiles, chained, *refs):
    refs = list(refs)
    x_ref, dy_ref, b_ref, c_ref, fsd_ref, ted_ref, e_ref, dxl_ref, pgb, pgc, pgl = refs[:11]
    refs = refs[11:]
    if chained:
        refs = refs[1:]
    dx_ref, gb_ref, gc_ref, gl_ref, gb, gc, later, early, jn = refs
    b = pl.program_id(0)
    j = pl.program_id(1)
    first = head0 + j * HPT
    rows = pl.ds(pl.multiple_of(b * BLOCK, BLOCK), BLOCK)

    @pl.when((b == 0) & (j == 0))
    def _():
        later[...] = jnp.zeros_like(later)
        early[...] = jnp.zeros_like(early)
        jn[...] = jnp.zeros_like(jn)

    @pl.when(j == 0)
    def _():
        gb[...] = pgb[...]
        gc[...] = pgc[...]

    oh2 = expander(first, 2, 6, TILE)
    pick = collector(first, TILE)
    te = expand(ted_ref[...], oh2)
    fs = expand(fsd_ref[...], oh2)
    ef = e_ref[:N]
    eb = e_ref[N:]
    sst = stack2(ef)
    gst = stack2(eb)
    bb = b_ref[...]
    cc = c_ref[...]
    x = x_ref[...].astype(F32)
    carried = te * mm(jnp.concatenate([bb, bb], axis=1), gst)
    read_out = mm(jnp.concatenate([cc, cc], axis=1), sst)
    dys = dy_ref[...].astype(F32) * fs
    dx_ref[...] = (dxl_ref[...] + carried).astype(BF16)
    early[rows, :] += collect(x * carried, pick)
    later[rows, :] += collect(dys * read_out, pick)
    gc[...] += contract_states(dys, sst)
    gb[...] += contract_states(x * te, gst)

    @pl.when(b == nb - 1)
    def _():
        v = fs[BLOCK - 1 : BLOCK] * jnp.sum(ef * eb, axis=0, keepdims=True)
        jn[...] += collect(jnp.broadcast_to(v, (8, TILE)), pick)

    @pl.when(j == tiles - 1)
    def _():
        gb_ref[...] = gb[...]
        gc_ref[...] = gc[...]

    @pl.when((b == nb - 1) & (j == tiles - 1))
    def _():
        before = tri(lambda a, r: r < a)
        onward = tri(lambda a, r: r >= a)
        hl = gl_ref.shape[0]
        blocks = [slice(i * BLOCK, (i + 1) * BLOCK) for i in range(nb)]
        lsum = [jnp.sum(later[s, :], axis=0, keepdims=True) for s in blocks]
        esum = [jnp.sum(early[s, :], axis=0, keepdims=True) for s in blocks]
        for i, s in enumerate(blocks):
            base = jn[0:1, :] + sum(esum[:i]) + sum(lsum[i + 1 :])
            glt = sum(mm(before, v) for v in split3(early[s, :])) + sum(mm(onward, v) for v in split3(later[s, :]))
            gl_ref[:, s] = pgl[:, s] + jnp.transpose(glt + base)[:hl]


def params():
    return pltpu.CompilerParams(vmem_limit_bytes=48 * 1024 * 1024)


SMEM = functools.partial(pl.BlockSpec, memory_space=pltpu.SMEM)
ANY = functools.partial(pl.BlockSpec, memory_space=pl.ANY)


def run_prep(lf, bounds, off):
    hl, tok = lf.shape
    shapes = [(tok, LANES), (hl, tok)] + [(tok, LANES)] * 4
    vmem = pl.BlockSpec(memory_space=pltpu.VMEM)
    return pl.pallas_call(
        functools.partial(prep_kernel, tok // BLOCK, bounds.shape[0]),
        out_shape=[jax.ShapeDtypeStruct(s, F32) for s in shapes],
        in_specs=[SMEM(), SMEM(), vmem],
        out_specs=[vmem] * 6,
        compiler_params=params(),
        cost_estimate=pl.CostEstimate(flops=10**8, bytes_accessed=4 * 10**6, transcendentals=10**6),
        name="prep",
    )(bounds, off, lf)


def run_summary(head0, cols, x, dy, b, c, fsb, teb):
    tok = x.shape[0]
    nb = tok // BLOCK
    t0 = head0 * P_SIZE // TILE
    tall = pl.BlockSpec((tok, TILE), lambda j: (0, t0 + j))
    full = pl.BlockSpec((tok, LANES), lambda j: (0, 0))
    return pl.pallas_call(
        functools.partial(summary_kernel, nb, head0),
        grid=(cols // TILE,),
        out_shape=[
            jax.ShapeDtypeStruct((2 * N + 8, cols), F32),
            jax.ShapeDtypeStruct((nb, 2 * N, cols), BF16),
            jax.ShapeDtypeStruct((nb, 2 * N, cols), BF16),
            jax.ShapeDtypeStruct((8, cols), F32),
        ],
        in_specs=[tall, tall, full, full, full, full],
        out_specs=[
            pl.BlockSpec((2 * N + 8, TILE), lambda j: (0, j)),
            pl.BlockSpec((nb, 2 * N, TILE), lambda j: (0, 0, j)),
            pl.BlockSpec((nb, 2 * N, TILE), lambda j: (0, 0, j)),
            pl.BlockSpec((8, TILE), lambda j: (0, j)),
        ],
        compiler_params=params(),
        cost_estimate=pl.CostEstimate(flops=8 * tok * N * cols, bytes_accessed=tok * cols * 12, transcendentals=0),
        name="summary",
    )(x, dy, b, c, fsb, teb)


def run_local(blk, head0, cols, args, carry, acc_in):
    bounds, off, x, dy, b, c, cumt, cumr, fsb, teb, sst, gst, jrow = args
    tok, wide = x.shape
    hl = cumr.shape[0]
    t0 = head0 * P_SIZE // TILE
    tiles = cols // TILE
    piece = pl.BlockSpec((BLOCK, TILE), lambda j: (blk, t0 + j))
    thin = pl.BlockSpec((BLOCK, LANES), lambda j: (blk, 0))
    hrow = pl.BlockSpec((hl, BLOCK), lambda j: (0, blk))
    st = pl.BlockSpec((1, 2 * N, TILE), lambda j: (blk, 0, j))
    in_specs = [SMEM(), SMEM(), piece, piece, thin, thin, thin, hrow, thin, thin, st, st]
    in_specs.append(pl.BlockSpec((8, TILE), lambda j: (0, j)))
    operands = list(args)
    aliases = {}
    if carry is not None:
        in_specs += [ANY(), thin, thin, hrow] if acc_in else [ANY()] * 4
        aliases = {len(operands) + i: i for i in range(4)}
        operands += list(carry)
    return pl.pallas_call(
        functools.partial(local_kernel, blk, head0, tiles, bounds.shape[0], carry is not None, acc_in),
        grid=(tiles,),
        out_shape=[
            jax.ShapeDtypeStruct((tok, wide), F32),
            jax.ShapeDtypeStruct((tok, N), F32),
            jax.ShapeDtypeStruct((tok, N), F32),
            jax.ShapeDtypeStruct((hl, tok), F32),
        ],
        in_specs=in_specs,
        out_specs=[piece, thin, thin, hrow],
        scratch_shapes=[
            pltpu.VMEM((BLOCK, BLOCK), F32),
            pltpu.VMEM((BLOCK, BLOCK), F32),
            pltpu.VMEM((BLOCK, N), F32),
            pltpu.VMEM((BLOCK, N), F32),
            pltpu.VMEM((BLOCK, LANES), F32),
            pltpu.VMEM((BLOCK, LANES), F32),
            pltpu.VMEM((hl, BLOCK), F32),
            pltpu.VMEM((8, LANES), F32),
        ],
        input_output_aliases=aliases,
        compiler_params=params(),
        cost_estimate=pl.CostEstimate(flops=24 * BLOCK * BLOCK * cols, bytes_accessed=BLOCK * cols * 12, transcendentals=BLOCK * BLOCK * cols // P_SIZE),
        name="local",
    )(*operands)


def run_enter(head0, cols, x, dy, b, c, fsd, ted, e, dxl, gb, gc, gl, dx_prev):
    tok, wide = x.shape
    nb = tok // BLOCK
    hl = gl.shape[0]
    t0 = head0 * P_SIZE // TILE
    tiles = cols // TILE
    piece = pl.BlockSpec((BLOCK, TILE), lambda i, j: (i, t0 + j))
    thin = pl.BlockSpec((BLOCK, LANES), lambda i, j: (i, 0))
    glf = pl.BlockSpec((hl, tok), lambda i, j: (0, 0))
    in_specs = [piece, piece, thin, thin, thin, thin, pl.BlockSpec((2 * N, TILE), lambda i, j: (0, j)), piece, thin, thin, glf]
    operands = [x, dy, b, c, fsd, ted, e, dxl, gb, gc, gl]
    aliases = {8: 1, 9: 2, 10: 3}
    if dx_prev is not None:
        in_specs.append(ANY())
        aliases[11] = 0
        operands.append(dx_prev)
    return pl.pallas_call(
        functools.partial(enter_kernel, nb, head0, tiles, dx_prev is not None),
        grid=(nb, tiles),
        out_shape=[
            jax.ShapeDtypeStruct((tok, wide), BF16),
            jax.ShapeDtypeStruct((tok, N), F32),
            jax.ShapeDtypeStruct((tok, N), F32),
            jax.ShapeDtypeStruct((hl, tok), F32),
        ],
        in_specs=in_specs,
        out_specs=[piece, thin, thin, glf],
        scratch_shapes=[
            pltpu.VMEM((BLOCK, N), F32),
            pltpu.VMEM((BLOCK, N), F32),
            pltpu.VMEM((tok, LANES), F32),
            pltpu.VMEM((tok, LANES), F32),
            pltpu.VMEM((8, LANES), F32),
        ],
        input_output_aliases=aliases,
        compiler_params=params(),
        cost_estimate=pl.CostEstimate(flops=20 * tok * N * cols, bytes_accessed=tok * cols * 12, transcendentals=0),
        name="enter",
    )(*operands)


def pick_by(index, options):
    out = options[0]
    for i in range(1, len(options)):
        out = jnp.where(index == i, options[i], out)
    return out


def parts_of(pay):
    return pay[:N], pay[N : 2 * N], pay[2 * N : 2 * N + 1]


def scan_over_seq(pay, n_seq, me):
    mid_n = n_seq // (2 * OUTER)
    core = me % 2
    mid = (me // 2) % mid_n
    cols = pay.shape[1]
    half = cols // 2
    w = half // mid_n

    def at(i):
        return i // (2 * mid_n), (i // 2) % mid_n, i % 2

    def index(o, m, c):
        return (o * mid_n + m) * 2 + c

    every = range(n_seq)
    swap = [(i, i ^ 1) for i in every]

    def mid_perm(s):
        return [(i, index(at(i)[0], (at(i)[1] + s) % mid_n, at(i)[2])) for i in every]

    def outer_perm(s):
        return [(i, i + s * 2 * mid_n) for i in every if 0 <= i + s * 2 * mid_n < n_seq]

    mine = lax.dynamic_slice_in_dim(pay, core * half, half, 1)
    theirs = lax.dynamic_slice_in_dim(pay, (1 - core) * half, half, 1)
    got = lax.ppermute(theirs, "seq", swap)
    f0, b0, d0 = parts_of(jnp.where(core == 0, mine, got))
    f1, b1, d1 = parts_of(jnp.where(core == 0, got, mine))
    chip = jnp.concatenate([d1 * f0 + f1, b0 + d0 * b1, jnp.broadcast_to(d0 * d1, (8, half))], axis=0)

    slices = [chip[:, q * w : (q + 1) * w] for q in range(mid_n)]
    own = pick_by(mid, slices)
    recv = [own] + [
        lax.ppermute(pick_by((mid + s) % mid_n, slices), "seq", mid_perm(s)) for s in range(1, mid_n)
    ]
    chips = [parts_of(pick_by((mid - q) % mid_n, recv)) for q in range(mid_n)]
    pf, pb, pd = chips[0]
    for f, b, d in chips[1:]:
        pf, pb, pd = d * pf + f, pb + pd * b, pd * d
    pd8 = jnp.broadcast_to(pd, (8, w))
    send_f = jnp.concatenate([pf, pd8], axis=0)
    send_b = jnp.concatenate([pb, pd8], axis=0)
    in_f = [lax.ppermute(send_f, "seq", outer_perm(s)) for s in range(1, OUTER)]
    in_b = [lax.ppermute(send_b, "seq", outer_perm(-s)) for s in range(1, OUTER)]

    def fold(arrived):
        acc = arrived[-1][:N]
        for v in arrived[-2::-1]:
            acc = v[:N] + v[N : N + 1] * acc
        return acc

    ef = fold(in_f)
    eb = fold(in_b)
    enter_f = []
    for f, b, d in chips:
        enter_f.append(ef)
        ef = d * ef + f
    enter_b = []
    for f, b, d in chips[::-1]:
        enter_b.append(eb)
        eb = b + d * eb
    enters = [jnp.concatenate(v, axis=0) for v in zip(enter_f, enter_b[::-1])]
    back = [pick_by(mid, enters)] + [
        lax.ppermute(pick_by((mid + s) % mid_n, enters), "seq", mid_perm(s)) for s in range(1, mid_n)
    ]
    chip_e = jnp.concatenate([pick_by((mid - q) % mid_n, back) for q in range(mid_n)], axis=1)
    cf, cb = chip_e[:N], chip_e[N:]
    first = jnp.concatenate([cf, b1 + d1 * cb], axis=0)
    second = jnp.concatenate([f0 + d0 * cf, cb], axis=0)
    keep = jnp.where(core == 0, first, second)
    got = lax.ppermute(jnp.where(core == 0, second, first), "seq", swap)
    return jnp.concatenate([jnp.where(core == 0, keep, got), jnp.where(core == 0, got, keep)], axis=1)


def sum_over_head(parts, n_head):
    me = lax.axis_index("head")
    cut = [v.reshape(n_head, -1, v.shape[1]) for v in parts]

    def piece(k):
        return jnp.concatenate([lax.dynamic_index_in_dim(v, k, 0, keepdims=False) for v in cut], axis=0)

    total = piece(me)
    for s in range(1, n_head):
        perm = [(i, (i + s) % n_head) for i in range(n_head)]
        total = total + lax.ppermute(piece((me + s) % n_head), "head", perm)
    rows = total.shape[0] // len(parts)
    return [total[i * rows : (i + 1) * rows] for i in range(len(parts))]


def on_device(n_seq, n_head, x, dy, b, c, lf, bounds):
    tok, wide = x.shape
    hl = lf.shape[0]
    nb = tok // BLOCK
    me = lax.axis_index("seq")
    off = (me * tok).astype(jnp.int32).reshape(1)
    groups = 2 if wide // 2 >= n_seq // OUTER * LANES else 1
    cols = wide // groups
    hg = hl // groups
    cumt, cumr, fsb, teb, fsd, ted = run_prep(lf, bounds, off)
    summaries = [run_summary(g * hg, cols, x, dy, b, c, fsb, teb) for g in range(groups)]
    enters = [scan_over_seq(s[0], n_seq, me) for s in summaries]
    carry = None
    for g in range(groups):
        _, sst, gst, jrow = summaries[g]
        for blk in range(nb):
            args = (bounds, off, x, dy, b, c, cumt, cumr, fsb, teb, sst, gst, jrow)
            carry = run_local(blk, g * hg, cols, args, carry, g > 0)
    dxl, gb, gc, gl = carry
    dx = None
    for g in range(groups):
        dx, gb, gc, gl = run_enter(g * hg, cols, x, dy, b, c, fsd, ted, enters[g], dxl, gb, gc, gl, dx)
    out_b, out_c = sum_over_head([gb, gc], n_head)
    return dx, out_b.astype(BF16), out_c.astype(BF16), gl


def solution(mesh):
    return jax.shard_map(
        functools.partial(on_device, mesh.shape["seq"], mesh.shape["head"]),
        mesh=mesh,
        in_specs=(
            P("seq", "head"),
            P("seq", "head"),
            P("seq", None),
            P("seq", None),
            P("head", "seq"),
            P(),
        ),
        out_specs=(
            P("seq", "head"),
            P(("seq", "head"), None),
            P(("seq", "head"), None),
            P("head", "seq"),
        ),
        check_vma=False,
    )
```

```python
import functools

import jax
import jax.numpy as jnp
from jax import lax
from jax.experimental import pallas as pl
from jax.experimental.pallas import tpu as pltpu
from jax.sharding import PartitionSpec as P

P_SIZE = 64
N = 128
BLOCK = 256
TILE = 256
HPT = TILE // P_SIZE
LANES = 128
OUTER = 4
LOG2E = 1.4426950408889634
F32 = jnp.float32
BF16 = jnp.bfloat16

NN = (((1,), (0,)), ((), ()))
NT = (((1,), (1,)), ((), ()))
TN = (((0,), (0,)), ((), ()))


def mm(a, b, dims=NN):
    return lax.dot_general(a, b, dims, preferred_element_type=F32)


def split2(v):
    hi = v.astype(BF16)
    return hi, (v - hi.astype(F32)).astype(BF16)


def split3(v):
    hi = v.astype(BF16)
    rest = v - hi.astype(F32)
    mid = rest.astype(BF16)
    return hi, mid, (rest - mid.astype(F32)).astype(BF16)


def iota2(shape, dim):
    return lax.broadcasted_iota(jnp.int32, shape, dim)


def ones_where(cond):
    return jnp.where(cond, 1.0, 0.0).astype(BF16)


def expander(first_head, parts, width_bits, cols):
    r = iota2((parts * LANES, cols), 0) & (LANES - 1)
    c = iota2((parts * LANES, cols), 1) >> width_bits
    return ones_where(r == c + first_head)


def collector(first_head, cols):
    c = iota2((cols, LANES), 0) >> 6
    h = iota2((cols, LANES), 1)
    return ones_where(h == c + first_head)


def expand(v, onehot2):
    hi, lo = split2(v)
    return mm(jnp.concatenate([hi, lo], axis=1), onehot2)


def collect(v, onehot):
    hi, lo = split2(v)
    return mm(hi, onehot) + mm(lo, onehot)


def tri(cond_of):
    return ones_where(cond_of(iota2((BLOCK, BLOCK), 0), iota2((BLOCK, BLOCK), 1)))


def prep_kernel(nb, nbounds, bounds, off, lf_ref, cumt_ref, cumr_ref, fsb_ref, teb_ref, fsd_ref, ted_ref):
    hl = lf_ref.shape[0]
    tok = nb * BLOCK
    lower = tri(lambda t, s: s <= t)
    upper = tri(lambda s, t: s <= t)
    run = jnp.zeros((1, LANES), F32)
    starts = []
    for b in range(nb):
        rows = slice(b * BLOCK, (b + 1) * BLOCK)
        lf = lf_ref[:, rows]
        lf_pad = jnp.concatenate([lf, jnp.zeros((LANES - hl, BLOCK), F32)], axis=0)
        parts = split3(lf_pad)
        cumt = sum(mm(lower, p, NT) for p in parts)
        cumr = sum(mm(p, upper) for p in parts)
        cumt_ref[rows, :] = cumt * LOG2E
        cumr_ref[:, rows] = cumr[:hl] * LOG2E
        starts.append(run)
        run = run + cumt[BLOCK - 1 : BLOCK]
    total = run
    t_loc = iota2((BLOCK, LANES), 0)
    for b in range(nb):
        rows = slice(b * BLOCK, (b + 1) * BLOCK)
        cumt = cumt_ref[rows, :] * (1.0 / LOG2E)
        last = cumt[BLOCK - 1 : BLOCK]
        t = t_loc + b * BLOCK
        cut_fb = jnp.zeros((BLOCK, LANES), jnp.bool_)
        cut_tb = cut_fb
        cut_fd = cut_fb
        cut_td = cut_fb
        for k in range(nbounds):
            bk = bounds[k] - off[0]
            cut_fd = cut_fd | ((bk >= 0) & (bk <= t))
            cut_td = cut_td | ((bk < tok) & (bk > t))
            cut_fb = cut_fb | ((bk >= b * BLOCK) & (bk <= t))
            cut_tb = cut_tb | ((bk < (b + 1) * BLOCK) & (bk > t))
        dev = starts[b] + cumt
        fsb_ref[rows, :] = jnp.where(cut_fb, 0.0, jnp.exp(cumt))
        teb_ref[rows, :] = jnp.where(cut_tb, 0.0, jnp.exp(jnp.minimum(last - cumt, 0.0)))
        fsd_ref[rows, :] = jnp.where(cut_fd, 0.0, jnp.exp(dev))
        ted_ref[rows, :] = jnp.where(cut_td, 0.0, jnp.exp(jnp.minimum(total - dev, 0.0)))


def stack2(v):
    hi, lo = split2(v)
    return jnp.concatenate([hi, lo], axis=0)


def summary_kernel(nb, head0, x_ref, dy_ref, b_ref, c_ref, fsb_ref, teb_ref, pay_ref, sst_ref, gst_ref, j_ref):
    first = head0 + pl.program_id(0) * HPT
    oh2 = expander(first, 2, 6, TILE)
    state = jnp.zeros((N, TILE), F32)
    states = []
    tots = []
    for b in range(nb):
        rows = slice(b * BLOCK, (b + 1) * BLOCK)
        states.append(state)
        sst_ref[b] = stack2(state)
        te = expand(teb_ref[rows, :], oh2)
        tot = expand(fsb_ref[(b + 1) * BLOCK - 8 : (b + 1) * BLOCK, :], oh2)[7:8]
        tots.append(tot)
        hi, lo = split2(x_ref[rows, :].astype(F32) * te)
        bb = b_ref[rows, :]
        state = tot * state + (mm(bb, hi, TN) + mm(bb, lo, TN))
    pay_ref[0:N] = state
    costate = jnp.zeros((N, TILE), F32)
    whole = jnp.ones((1, TILE), F32)
    for b in reversed(range(nb)):
        rows = slice(b * BLOCK, (b + 1) * BLOCK)
        gst_ref[b] = stack2(costate)
        j_ref[b : b + 1, :] = tots[b] * jnp.sum(states[b] * costate, axis=0, keepdims=True)
        fs = expand(fsb_ref[rows, :], oh2)
        hi, lo = split2(dy_ref[rows, :].astype(F32) * fs)
        cc = c_ref[rows, :]
        costate = tots[b] * costate + (mm(cc, hi, TN) + mm(cc, lo, TN))
        whole = whole * tots[b]
    pay_ref[N : 2 * N] = costate
    pay_ref[2 * N : 2 * N + 8] = jnp.broadcast_to(whole, (8, TILE))
    for b in range(nb, j_ref.shape[0]):
        j_ref[b : b + 1, :] = jnp.zeros((1, TILE), F32)


def contract_states(scaled, stacked):
    hi, lo = split2(scaled)
    both = mm(hi, stacked, NT)
    return both[:, :N] + both[:, N:] + mm(lo, stacked[:N], NT)


def local_kernel(blk, head0, tiles, nbounds, chained, own_dx, acc_in, *refs):
    refs = list(refs)
    bounds, off = refs[:2]
    x_ref, dy_ref, b_ref, c_ref, cumt_ref, cumr_ref, fsb_ref, teb_ref, sst_ref, gst_ref, j_ref = refs[2:13]
    refs = refs[13:]
    if chained:
        prev_gb, prev_gc, prev_gl = refs[:3]
        refs = refs[4:] if own_dx else refs[3:]
    dx_ref, gb_ref, gc_ref, gl_ref, gt, wt, gb, gc, later, col, rows_s, jn = refs
    j = pl.program_id(0)
    first = head0 + j * HPT
    half = BLOCK // 2

    @pl.when(j == 0)
    def _():
        s = iota2((BLOCK, BLOCK), 0)
        t = iota2((BLOCK, BLOCK), 1)
        ok = s <= t
        for k in range(nbounds):
            bk = bounds[k] - off[0] - blk * BLOCK
            ok = ok & ((s >= bk) | (t < bk))
        gt[...] = jnp.where(ok, mm(b_ref[...], c_ref[...], NT), 0.0)
        wt[...] = jnp.zeros_like(wt)
        gb[...] = prev_gb[...] if acc_in else jnp.zeros_like(gb)
        gc[...] = prev_gc[...] if acc_in else jnp.zeros_like(gc)
        later[...] = jnp.zeros_like(later)
        col[...] = jnp.zeros_like(col)
        rows_s[...] = jnp.zeros_like(rows_s)
        jn[...] = jnp.zeros_like(jn)

    oh2 = expander(first, 2, 6, TILE)
    te = expand(teb_ref[...], oh2)
    fs = expand(fsb_ref[...], oh2)
    sst = sst_ref[0]
    gst = gst_ref[0]
    bb = b_ref[...]
    cc = c_ref[...]
    carried = te * mm(jnp.concatenate([bb, bb], axis=1), gst)
    read_out = mm(jnp.concatenate([cc, cc], axis=1), sst)
    colb = mm(jnp.concatenate(split3(cumt_ref[...]), axis=1), expander(first, 3, 7, HPT * LANES))
    low_lane = iota2((BLOCK, LANES), 1) < P_SIZE
    for p in range(HPT // 2):
        lanes = slice(p * LANES, (p + 1) * LANES)
        xp = x_ref[:, lanes]
        dyp = dy_ref[:, lanes]
        top = carried[:half, lanes]
        bot = carried[half:, lanes]
        for q in range(2):
            k = 2 * p + q
            dym = jnp.where(low_lane if q == 0 else ~low_lane, dyp, jnp.zeros_like(dyp))
            p0 = mm(xp[:half], dym, NT)
            p1 = mm(xp[half:], dym[half:], NT)
            cr = cumr_ref[pl.ds(first + k, 1), :]
            cb = colb[:, k * LANES : (k + 1) * LANES]
            d00 = jnp.exp2(jnp.minimum(cr[:, :half] - cb[:half], 0.0))
            d01 = jnp.exp2(jnp.minimum(cr[:, half:] - cb[:half], 0.0))
            d11 = jnp.exp2(jnp.minimum(cr[:, half:] - cb[half:], 0.0))
            a00 = p0[:, :half] * d00
            a01 = p0[:, half:] * d01
            a11 = p1 * d11
            wt[:half, :half] += a00
            wt[:half, half:] += a01
            wt[half:, half:] += a11
            g00 = gt[:half, :half]
            g01 = gt[:half, half:]
            g11 = gt[half:, half:]
            rows_s[pl.ds(first + k, 1), :] = jnp.concatenate(
                [
                    jnp.sum(a00 * g00, axis=0, keepdims=True),
                    jnp.sum(a01 * g01 + a11 * g11, axis=0, keepdims=True),
                ],
                axis=1,
            )
            h00, l00 = split2(d00 * g00)
            h01, l01 = split2(d01 * g01)
            h11, l11 = split2(d11 * g11)
            top = top + mm(jnp.concatenate([h00, h01], axis=1), dym)
            top = top + mm(jnp.concatenate([l00, l01], axis=1), dym)
            bot = bot + mm(jnp.concatenate([h11, l11], axis=1), jnp.concatenate([dym[half:], dym[half:]], axis=0))
        dx_ref[:half, lanes] = top
        dx_ref[half:, lanes] = bot
    pick = collector(first, TILE)
    x = x_ref[...].astype(F32)
    dys = dy_ref[...].astype(F32) * fs
    col[...] += collect(x * dx_ref[...], pick)
    later[...] += collect(dys * read_out, pick)
    gc[...] += contract_states(dys, sst)
    gb[...] += contract_states(x * te, gst)
    jn[...] += collect(jnp.broadcast_to(j_ref[blk : blk + 1, :], (8, TILE)), pick)

    @pl.when(j == tiles - 1)
    def _():
        s = iota2((BLOCK, BLOCK), 0)
        t = iota2((BLOCK, BLOCK), 1)
        ok = s <= t
        for k in range(nbounds):
            bk = bounds[k] - off[0] - blk * BLOCK
            ok = ok & ((s >= bk) | (t < bk))
        hi, lo = split2(jnp.where(ok, wt[...], 0.0))
        gb_ref[...] = gb[...] + mm(hi, cc) + mm(lo, cc)
        gc_ref[...] = gc[...] + mm(hi, bb, TN) + mm(lo, bb, TN)
        before = tri(lambda a, r: r < a)
        onward = tri(lambda a, r: r >= a)
        upper = tri(lambda r, a: r < a)
        glt = sum(mm(before, v) for v in split3(col[...])) + sum(mm(onward, v) for v in split3(later[...]))
        glt = glt + jn[0:1, :]
        rows_cum = sum(mm(v, upper) for v in split3(rows_s[...]))
        gl = jnp.transpose(glt)[: rows_s.shape[0]] - rows_cum
        gl_ref[...] = gl + prev_gl[...] if acc_in else gl


def enter_kernel(nb, head0, tiles, chained, *refs):
    refs = list(refs)
    x_ref, dy_ref, b_ref, c_ref, fsd_ref, ted_ref, e_ref, dxl_ref, pgb, pgc, pgl = refs[:11]
    refs = refs[11:]
    if chained:
        refs = refs[1:]
    dx_ref, gb_ref, gc_ref, gl_ref, gb, gc, later, early, jn = refs
    b = pl.program_id(0)
    j = pl.program_id(1)
    first = head0 + j * HPT
    rows = pl.ds(pl.multiple_of(b * BLOCK, BLOCK), BLOCK)

    @pl.when((b == 0) & (j == 0))
    def _():
        later[...] = jnp.zeros_like(later)
        early[...] = jnp.zeros_like(early)
        jn[...] = jnp.zeros_like(jn)

    @pl.when(j == 0)
    def _():
        gb[...] = pgb[...]
        gc[...] = pgc[...]

    oh2 = expander(first, 2, 6, TILE)
    pick = collector(first, TILE)
    te = expand(ted_ref[...], oh2)
    fs = expand(fsd_ref[...], oh2)
    ef = e_ref[:N]
    eb = e_ref[N:]
    sst = stack2(ef)
    gst = stack2(eb)
    bb = b_ref[...]
    cc = c_ref[...]
    x = x_ref[...].astype(F32)
    carried = te * mm(jnp.concatenate([bb, bb], axis=1), gst)
    read_out = mm(jnp.concatenate([cc, cc], axis=1), sst)
    dys = dy_ref[...].astype(F32) * fs
    dx_ref[...] = (dxl_ref[...] + carried).astype(BF16)
    early[rows, :] += collect(x * carried, pick)
    later[rows, :] += collect(dys * read_out, pick)
    gc[...] += contract_states(dys, sst)
    gb[...] += contract_states(x * te, gst)

    @pl.when(b == nb - 1)
    def _():
        v = fs[BLOCK - 1 : BLOCK] * jnp.sum(ef * eb, axis=0, keepdims=True)
        jn[...] += collect(jnp.broadcast_to(v, (8, TILE)), pick)

    @pl.when(j == tiles - 1)
    def _():
        gb_ref[...] = gb[...]
        gc_ref[...] = gc[...]

    @pl.when((b == nb - 1) & (j == tiles - 1))
    def _():
        before = tri(lambda a, r: r < a)
        onward = tri(lambda a, r: r >= a)
        hl = gl_ref.shape[0]
        blocks = [slice(i * BLOCK, (i + 1) * BLOCK) for i in range(nb)]
        lsum = [jnp.sum(later[s, :], axis=0, keepdims=True) for s in blocks]
        esum = [jnp.sum(early[s, :], axis=0, keepdims=True) for s in blocks]
        for i, s in enumerate(blocks):
            base = jn[0:1, :] + sum(esum[:i]) + sum(lsum[i + 1 :])
            glt = sum(mm(before, v) for v in split3(early[s, :])) + sum(mm(onward, v) for v in split3(later[s, :]))
            gl_ref[:, s] = pgl[:, s] + jnp.transpose(glt + base)[:hl]


def params():
    return pltpu.CompilerParams(vmem_limit_bytes=58 * 1024 * 1024)


SMEM = functools.partial(pl.BlockSpec, memory_space=pltpu.SMEM)
ANY = functools.partial(pl.BlockSpec, memory_space=pl.ANY)


def run_prep(lf, bounds, off):
    hl, tok = lf.shape
    shapes = [(tok, LANES), (hl, tok)] + [(tok, LANES)] * 4
    vmem = pl.BlockSpec(memory_space=pltpu.VMEM)
    return pl.pallas_call(
        functools.partial(prep_kernel, tok // BLOCK, bounds.shape[0]),
        out_shape=[jax.ShapeDtypeStruct(s, F32) for s in shapes],
        in_specs=[SMEM(), SMEM(), vmem],
        out_specs=[vmem] * 6,
        compiler_params=params(),
        cost_estimate=pl.CostEstimate(flops=10**8, bytes_accessed=4 * 10**6, transcendentals=10**6),
        name="prep",
    )(bounds, off, lf)


def run_summary(head0, cols, x, dy, b, c, fsb, teb):
    tok = x.shape[0]
    nb = tok // BLOCK
    t0 = head0 * P_SIZE // TILE
    tall = pl.BlockSpec((tok, TILE), lambda j: (0, t0 + j))
    full = pl.BlockSpec((tok, LANES), lambda j: (0, 0))
    return pl.pallas_call(
        functools.partial(summary_kernel, nb, head0),
        grid=(cols // TILE,),
        out_shape=[
            jax.ShapeDtypeStruct((2 * N + 8, cols), F32),
            jax.ShapeDtypeStruct((nb, 2 * N, cols), BF16),
            jax.ShapeDtypeStruct((nb, 2 * N, cols), BF16),
            jax.ShapeDtypeStruct((8, cols), F32),
        ],
        in_specs=[tall, tall, full, full, full, full],
        out_specs=[
            pl.BlockSpec((2 * N + 8, TILE), lambda j: (0, j)),
            pl.BlockSpec((nb, 2 * N, TILE), lambda j: (0, 0, j)),
            pl.BlockSpec((nb, 2 * N, TILE), lambda j: (0, 0, j)),
            pl.BlockSpec((8, TILE), lambda j: (0, j)),
        ],
        compiler_params=params(),
        cost_estimate=pl.CostEstimate(flops=8 * tok * N * cols, bytes_accessed=tok * cols * 12, transcendentals=0),
        name="summary",
    )(x, dy, b, c, fsb, teb)


def run_local(blk, head0, cols, args, dxl, carry, acc_in):
    bounds, off, x, dy, b, c, cumt, cumr, fsb, teb, sst, gst, jrow = args
    tok = x.shape[0]
    hl = cumr.shape[0]
    t0 = head0 * P_SIZE // TILE
    tiles = cols // TILE
    piece = pl.BlockSpec((BLOCK, TILE), lambda j: (blk, t0 + j))
    piece_out = pl.BlockSpec((BLOCK, TILE), lambda j: (blk, j))
    thin = pl.BlockSpec((BLOCK, LANES), lambda j: (blk, 0))
    hrow = pl.BlockSpec((hl, BLOCK), lambda j: (0, blk))
    st = pl.BlockSpec((1, 2 * N, TILE), lambda j: (blk, 0, j))
    in_specs = [SMEM(), SMEM(), piece, piece, thin, thin, thin, hrow, thin, thin, st, st]
    in_specs.append(pl.BlockSpec((8, TILE), lambda j: (0, j)))
    operands = list(args)
    aliases = {}
    if carry is not None:
        in_specs += [thin, thin, hrow] if acc_in else [ANY()] * 3
        aliases = {len(operands) + i: 1 + i for i in range(3)}
        operands += list(carry)
        if dxl is not None:
            aliases[len(operands)] = 0
            in_specs.append(ANY())
            operands.append(dxl)
    out = pl.pallas_call(
        functools.partial(
            local_kernel, blk, head0, tiles, bounds.shape[0], carry is not None, dxl is not None, acc_in
        ),
        grid=(tiles,),
        out_shape=[
            jax.ShapeDtypeStruct((tok, cols), F32),
            jax.ShapeDtypeStruct((tok, N), F32),
            jax.ShapeDtypeStruct((tok, N), F32),
            jax.ShapeDtypeStruct((hl, tok), F32),
        ],
        in_specs=in_specs,
        out_specs=[piece_out, thin, thin, hrow],
        scratch_shapes=[
            pltpu.VMEM((BLOCK, BLOCK), F32),
            pltpu.VMEM((BLOCK, BLOCK), F32),
            pltpu.VMEM((BLOCK, N), F32),
            pltpu.VMEM((BLOCK, N), F32),
            pltpu.VMEM((BLOCK, LANES), F32),
            pltpu.VMEM((BLOCK, LANES), F32),
            pltpu.VMEM((hl, BLOCK), F32),
            pltpu.VMEM((8, LANES), F32),
        ],
        input_output_aliases=aliases,
        compiler_params=params(),
        cost_estimate=pl.CostEstimate(
            flops=24 * BLOCK * BLOCK * cols, bytes_accessed=BLOCK * cols * 12, transcendentals=0
        ),
        name="local",
    )(*operands)
    return out[0], tuple(out[1:])


def run_enter(head0, cols, x, dy, b, c, fsd, ted, e, dxl, gb, gc, gl, dx_prev):
    tok, wide = x.shape
    nb = tok // BLOCK
    hl = gl.shape[0]
    t0 = head0 * P_SIZE // TILE
    tiles = cols // TILE
    piece = pl.BlockSpec((BLOCK, TILE), lambda i, j: (i, t0 + j))
    own = pl.BlockSpec((BLOCK, TILE), lambda i, j: (i, j))
    thin = pl.BlockSpec((BLOCK, LANES), lambda i, j: (i, 0))
    glf = pl.BlockSpec((hl, tok), lambda i, j: (0, 0))
    in_specs = [piece, piece, thin, thin, thin, thin, pl.BlockSpec((2 * N, TILE), lambda i, j: (0, j)), own, thin, thin, glf]
    operands = [x, dy, b, c, fsd, ted, e, dxl, gb, gc, gl]
    aliases = {8: 1, 9: 2, 10: 3}
    if dx_prev is not None:
        in_specs.append(ANY())
        aliases[11] = 0
        operands.append(dx_prev)
    return pl.pallas_call(
        functools.partial(enter_kernel, nb, head0, tiles, dx_prev is not None),
        grid=(nb, tiles),
        out_shape=[
            jax.ShapeDtypeStruct((tok, wide), BF16),
            jax.ShapeDtypeStruct((tok, N), F32),
            jax.ShapeDtypeStruct((tok, N), F32),
            jax.ShapeDtypeStruct((hl, tok), F32),
        ],
        in_specs=in_specs,
        out_specs=[piece, thin, thin, glf],
        scratch_shapes=[
            pltpu.VMEM((BLOCK, N), F32),
            pltpu.VMEM((BLOCK, N), F32),
            pltpu.VMEM((tok, LANES), F32),
            pltpu.VMEM((tok, LANES), F32),
            pltpu.VMEM((8, LANES), F32),
        ],
        input_output_aliases=aliases,
        compiler_params=params(),
        cost_estimate=pl.CostEstimate(flops=20 * tok * N * cols, bytes_accessed=tok * cols * 12, transcendentals=0),
        name="enter",
    )(*operands)


def pick_by(index, options):
    out = options[0]
    for i in range(1, len(options)):
        out = jnp.where(index == i, options[i], out)
    return out


def parts_of(pay):
    return pay[:N], pay[N : 2 * N], pay[2 * N : 2 * N + 1]


def scan_over_seq(pay, n_seq, me):
    mid_n = n_seq // (2 * OUTER)
    core = me % 2
    mid = (me // 2) % mid_n
    cols = pay.shape[1]
    half = cols // 2
    w = half // mid_n

    def at(i):
        return i // (2 * mid_n), (i // 2) % mid_n, i % 2

    def index(o, m, c):
        return (o * mid_n + m) * 2 + c

    every = range(n_seq)
    swap = [(i, i ^ 1) for i in every]

    def mid_perm(s):
        return [(i, index(at(i)[0], (at(i)[1] + s) % mid_n, at(i)[2])) for i in every]

    def outer_perm(s):
        return [(i, (i + s * 2 * mid_n) % n_seq) for i in every]

    mine = lax.dynamic_slice_in_dim(pay, core * half, half, 1)
    theirs = lax.dynamic_slice_in_dim(pay, (1 - core) * half, half, 1)
    (got,) = yield [(theirs, swap)]
    f0, b0, d0 = parts_of(jnp.where(core == 0, mine, got))
    f1, b1, d1 = parts_of(jnp.where(core == 0, got, mine))
    chip = jnp.concatenate([d1 * f0 + f1, b0 + d0 * b1, jnp.broadcast_to(d0 * d1, (8, half))], axis=0)

    slices = [chip[:, q * w : (q + 1) * w] for q in range(mid_n)]
    own = pick_by(mid, slices)
    got = yield [(pick_by((mid + s) % mid_n, slices), mid_perm(s)) for s in range(1, mid_n)]
    recv = [own] + got
    chips = [parts_of(pick_by((mid - q) % mid_n, recv)) for q in range(mid_n)]
    pf, pb, pd = chips[0]
    for f, b, d in chips[1:]:
        pf, pb, pd = d * pf + f, pb + pd * b, pd * d
    outer = me // (2 * mid_n)
    pd8 = jnp.broadcast_to(pd, (8, w))
    sends = []
    for s in range(1, OUTER):
        up = outer + s < OUTER
        sends.append((jnp.concatenate([jnp.where(up, pf, pb), pd8], axis=0), outer_perm(s)))
    got = yield sends

    def fold(arrived, reach):
        acc = jnp.zeros((N, w), F32)
        for s in range(OUTER - 1, 0, -1):
            v = arrived[s - 1]
            acc = jnp.where(s <= reach, v[:N] + v[N : N + 1] * acc, 0.0)
        return acc

    ef = fold(got, outer)
    eb = fold(got[::-1], OUTER - 1 - outer)
    enter_f = []
    for f, b, d in chips:
        enter_f.append(ef)
        ef = d * ef + f
    enter_b = []
    for f, b, d in chips[::-1]:
        enter_b.append(eb)
        eb = b + d * eb
    enters = [jnp.concatenate(v, axis=0) for v in zip(enter_f, enter_b[::-1])]
    got = yield [(pick_by((mid + s) % mid_n, enters), mid_perm(s)) for s in range(1, mid_n)]
    back = [pick_by(mid, enters)] + got
    chip_e = jnp.concatenate([pick_by((mid - q) % mid_n, back) for q in range(mid_n)], axis=1)
    cf, cb = chip_e[:N], chip_e[N:]
    first = jnp.concatenate([cf, b1 + d1 * cb], axis=0)
    second = jnp.concatenate([f0 + d0 * cf, cb], axis=0)
    keep = jnp.where(core == 0, first, second)
    (got,) = yield [(jnp.where(core == 0, second, first), swap)]
    yield jnp.concatenate([jnp.where(core == 0, keep, got), jnp.where(core == 0, got, keep)], axis=1)


def sum_over_head(parts, n_head):
    me = lax.axis_index("head")
    cut = [v.reshape(n_head, -1, v.shape[1]) for v in parts]

    def piece(k):
        return jnp.concatenate([lax.dynamic_index_in_dim(v, k, 0, keepdims=False) for v in cut], axis=0)

    total = piece(me)
    for s in range(1, n_head):
        perm = [(i, (i + s) % n_head) for i in range(n_head)]
        total = total + lax.ppermute(piece((me + s) % n_head), "head", perm)
    rows = total.shape[0] // len(parts)
    return [total[i * rows : (i + 1) * rows] for i in range(len(parts))]


def on_device(n_seq, n_head, x, dy, b, c, lf, bounds):
    tok, wide = x.shape
    hl = lf.shape[0]
    nb = tok // BLOCK
    me = lax.axis_index("seq")
    off = (me * tok).astype(jnp.int32).reshape(1)
    groups = 2 if wide // 2 >= n_seq // OUTER * LANES else 1
    cols = wide // groups
    hg = hl // groups
    cumt, cumr, fsb, teb, fsd, ted = run_prep(lf, bounds, off)
    dxl = [None] * groups
    sums = [None] * groups
    scans = [None] * groups
    enters = [None] * groups
    sends = [None] * groups
    todo = [(g, blk) for g in range(groups) for blk in range(nb)]
    carry = None
    dx = None

    def summarise(g, gate):
        summed = run_summary(g * hg, cols, gate, dy, b, c, fsb, teb)
        sums[g] = summed[1:]
        scans[g] = scan_over_seq(summed[0], n_seq, me)
        sends[g] = next(scans[g])

    def local_piece():
        nonlocal carry
        g, blk = todo.pop(0)
        args = (bounds, off, x, dy, b, c, cumt, cumr, fsb, teb, *sums[g])
        dxl[g], carry = run_local(blk, g * hg, cols, args, dxl[g], carry, g > 0)

    def fly(moving):
        return [[lax.ppermute(v, "seq", p) for v, p in sends[g]] for g in moving]

    def land(moving, arrived):
        nonlocal carry
        if carry is not None:
            arrived, carry = lax.optimization_barrier((arrived, carry))
        for g, got in zip(moving, arrived):
            out = scans[g].send(got)
            if isinstance(out, list):
                sends[g] = out
            else:
                enters[g] = out
                sends[g] = None

    def enter(g):
        nonlocal carry, dx
        dx, *new = run_enter(g * hg, cols, x, dy, b, c, fsd, ted, enters[g], dxl[g], *carry, dx)
        carry = tuple(new)

    summarise(0, x)
    if groups == 1:
        for pieces in (1, 1, 2, 0, 0):
            arrived = fly([0])
            for _ in range(pieces):
                local_piece()
            land([0], arrived)
        enter(0)
    else:
        arrived = fly([0])
        summarise(1, x)
        land([0], arrived)
        for moving, pieces in (([0, 1], 1), ([0, 1], 2), ([0, 1], 2), ([0, 1], 1), ([1], 1)):
            arrived = fly(moving)
            for _ in range(pieces):
                local_piece()
            land(moving, arrived)
        while todo:
            local_piece()
        enter(0)
        enter(1)
    gb, gc, gl = carry
    out_b, out_c = sum_over_head([gb, gc], n_head)
    return dx, out_b.astype(BF16), out_c.astype(BF16), gl


def solution(mesh):
    return jax.shard_map(
        functools.partial(on_device, mesh.shape["seq"], mesh.shape["head"]),
        mesh=mesh,
        in_specs=(
            P("seq", "head"),
            P("seq", "head"),
            P("seq", None),
            P("seq", None),
            P("head", "seq"),
            P(),
        ),
        out_specs=(
            P("seq", "head"),
            P(("seq", "head"), None),
            P(("seq", "head"), None),
            P("head", "seq"),
        ),
        check_vma=False,
    )
```

```python
import functools

import jax
import jax.numpy as jnp
from jax import lax
from jax.experimental import pallas as pl
from jax.experimental.pallas import tpu as pltpu
from jax.sharding import PartitionSpec as P

P_SIZE = 64
N = 128
BLOCK = 256
TILE = 256
HPT = TILE // P_SIZE
LANES = 128
OUTER = 4
LOG2E = 1.4426950408889634
F32 = jnp.float32
BF16 = jnp.bfloat16

NN = (((1,), (0,)), ((), ()))
NT = (((1,), (1,)), ((), ()))
TN = (((0,), (0,)), ((), ()))


def mm(a, b, dims=NN):
    return lax.dot_general(a, b, dims, preferred_element_type=F32)


def split2(v):
    hi = v.astype(BF16)
    return hi, (v - hi.astype(F32)).astype(BF16)


def split3(v):
    hi = v.astype(BF16)
    rest = v - hi.astype(F32)
    mid = rest.astype(BF16)
    return hi, mid, (rest - mid.astype(F32)).astype(BF16)


def iota2(shape, dim):
    return lax.broadcasted_iota(jnp.int32, shape, dim)


def ones_where(cond):
    return jnp.where(cond, 1.0, 0.0).astype(BF16)


def expander(first_head, cols):
    r = iota2((2 * LANES, cols), 0) & (LANES - 1)
    c = iota2((2 * LANES, cols), 1) >> 6
    return ones_where(r == c + first_head)


def collector(cols):
    c = iota2((cols, LANES), 0) >> 6
    h = iota2((cols, LANES), 1)
    return ones_where(h == c)


def side_by_side(v):
    return jnp.concatenate(split2(v), axis=1)


def stack2(v):
    return jnp.concatenate(split2(v), axis=0)


def collect(v, onehot):
    hi, lo = split2(v)
    return mm(hi, onehot) + mm(lo, onehot)


def contract_states(scaled, stacked):
    hi, lo = split2(scaled)
    both = mm(hi, stacked, NT)
    return both[:, :N] + both[:, N:] + mm(lo, stacked[:N], NT)


def tri(cond_of):
    return ones_where(cond_of(iota2((BLOCK, BLOCK), 0), iota2((BLOCK, BLOCK), 1)))


def prep_kernel(nb, nbounds, bounds, off, lf_ref, cumt_ref, cumr_ref, fsb_ref, teb_ref, edge_ref):
    hl = lf_ref.shape[0]
    tok = nb * BLOCK
    lower = tri(lambda t, s: s <= t)
    upper = tri(lambda s, t: s <= t)
    local = [bounds[k] - off[0] for k in range(nbounds)]

    def first_from(start):
        out = tok
        for v in local:
            out = jnp.minimum(out, jnp.where(v >= start, v, tok))
        return out

    def last_before(end):
        out = -1
        for v in local:
            out = jnp.maximum(out, jnp.where(v < end, v, -1))
        return out

    t_loc = iota2((BLOCK, LANES), 0)
    lasts = []
    for b in range(nb):
        rows = slice(b * BLOCK, (b + 1) * BLOCK)
        lf_pad = jnp.concatenate([lf_ref[:, rows], jnp.zeros((LANES - hl, BLOCK), F32)], axis=0)
        parts = split3(lf_pad)
        cumt = sum(mm(lower, p, NT) for p in parts)
        cumr = sum(mm(p, upper) for p in parts)
        cumt_ref[rows, :] = cumt * LOG2E
        cumr_ref[:, rows] = cumr[:hl] * LOG2E
        last = cumt[BLOCK - 1 : BLOCK]
        lasts.append(last)
        t = t_loc + b * BLOCK
        fsb_ref[rows, :] = jnp.where(t >= first_from(b * BLOCK), 0.0, jnp.exp(cumt))
        teb_ref[rows, :] = jnp.where(
            t < last_before((b + 1) * BLOCK), 0.0, jnp.exp(jnp.minimum(last - cumt, 0.0))
        )
    zero = jnp.zeros((1, LANES), F32)
    first = first_from(0)
    final = last_before(tok)
    for b in range(8):
        if b < nb:
            into = jnp.exp(sum(lasts[:b], zero))
            outof = jnp.exp(sum(lasts[b + 1 :], zero))
            edge_ref[b : b + 1, :] = jnp.where(first >= b * BLOCK, into, 0.0)
            edge_ref[8 + b : 9 + b, :] = jnp.where(final < (b + 1) * BLOCK, outof, 0.0)
        else:
            edge_ref[b : b + 1, :] = zero
            edge_ref[8 + b : 9 + b, :] = zero


def summary_kernel(nb, head0, x_ref, dy_ref, b_ref, c_ref, fsb_ref, teb_ref, pay_ref, st_ref, co_ref):
    oh2 = expander(head0 + pl.program_id(0) * HPT, TILE)
    state = jnp.zeros((N, TILE), F32)
    costate = jnp.zeros((N, TILE), F32)
    whole = jnp.ones((1, TILE), F32)
    tots = [
        mm(side_by_side(fsb_ref[(b + 1) * BLOCK - 8 : (b + 1) * BLOCK, :]), oh2)[7:8] for b in range(nb)
    ]
    for b in range(nb):
        rows = slice(b * BLOCK, (b + 1) * BLOCK)
        st_ref[b] = state
        te = mm(side_by_side(teb_ref[rows, :]), oh2)
        hi, lo = split2(x_ref[rows, :].astype(F32) * te)
        bb = b_ref[rows, :]
        state = tots[b] * state + (mm(bb, hi, TN) + mm(bb, lo, TN))
        r = nb - 1 - b
        rows = slice(r * BLOCK, (r + 1) * BLOCK)
        co_ref[r] = costate
        fs = mm(side_by_side(fsb_ref[rows, :]), oh2)
        hi, lo = split2(dy_ref[rows, :].astype(F32) * fs)
        cc = c_ref[rows, :]
        costate = tots[r] * costate + (mm(cc, hi, TN) + mm(cc, lo, TN))
        whole = whole * tots[b]
    pay_ref[0:N] = state
    pay_ref[N : 2 * N] = costate
    pay_ref[2 * N : 2 * N + 8] = jnp.broadcast_to(whole, (8, TILE))


def local_kernel(blk0, head0, nbounds, chained, *refs):
    refs = list(refs)
    bounds, off, x_ref, dy_ref, b_ref, c_ref, cumt_ref, cumr_ref = refs[:8]
    dx_ref, wb_ref, wc_ref, rows_ref, gt, wt, rows_s = refs[12:] if chained else refs[8:]
    start = off[0] + (blk0 + pl.program_id(0)) * BLOCK
    half = BLOCK // 2
    pairs = x_ref.shape[1] // LANES

    def segments(shape, dim):
        pos = iota2(shape, dim) + start
        seg = jnp.zeros(shape, jnp.int32)
        for k in range(nbounds):
            seg = seg + jnp.where(pos >= bounds[k], 1, 0)
        return seg

    ok = (segments((BLOCK, 1), 0) == segments((1, BLOCK), 1)) & (
        iota2((BLOCK, BLOCK), 0) <= iota2((BLOCK, BLOCK), 1)
    )
    bb = b_ref[...]
    cc = c_ref[...]
    gt[...] = jnp.where(ok, mm(bb, cc, NT), 0.0)
    wt[...] = jnp.zeros_like(wt)
    low_lane = iota2((BLOCK, LANES), 1) < P_SIZE
    for p in range(pairs):
        lanes = slice(p * LANES, (p + 1) * LANES)
        xp = x_ref[:, lanes]
        dyp = dy_ref[:, lanes]
        none = jnp.zeros_like(xp)
        picked = jnp.concatenate([jnp.where(low_lane, xp, none), jnp.where(low_lane, none, xp)], axis=0)
        prod = mm(picked, dyp, NT)
        tops = []
        bots = []
        acc = None
        for q in range(2):
            k = 2 * p + q
            pq = prod[q * BLOCK : (q + 1) * BLOCK]
            cr = cumr_ref[k : k + 1, :]
            cb = jnp.broadcast_to(cumt_ref[:, head0 + k : head0 + k + 1], (BLOCK, half))
            d00 = jnp.exp2(jnp.minimum(cr[:, :half] - cb[:half], 0.0))
            d01 = jnp.exp2(cr[:, half:] - cb[:half])
            d11 = jnp.exp2(jnp.minimum(cr[:, half:] - cb[half:], 0.0))
            a00 = pq[:half, :half] * d00
            a01 = pq[:half, half:] * d01
            a11 = pq[half:, half:] * d11
            acc = (a00, a01, a11) if q == 0 else (acc[0] + a00, acc[1] + a01, acc[2] + a11)
            g00 = gt[:half, :half]
            g01 = gt[:half, half:]
            g11 = gt[half:, half:]
            rows_s[k : k + 1, :half] = jnp.sum(a00 * g00, axis=0, keepdims=True)
            rows_s[k : k + 1, half:] = jnp.sum(a01 * g01 + a11 * g11, axis=0, keepdims=True)
            h00, l00 = split2(d00 * g00)
            h01, l01 = split2(d01 * g01)
            h11, l11 = split2(d11 * g11)
            tops.append(jnp.concatenate([h00, h01, l00, l01], axis=1))
            bots.append(jnp.concatenate([h11, l11], axis=1))
        wt[:half, :half] += acc[0]
        wt[:half, half:] += acc[1]
        wt[half:, half:] += acc[2]
        dyh = dyp[half:]
        top = mm(jnp.concatenate(tops, axis=0), jnp.concatenate([dyp, dyp], axis=0))
        bot = mm(jnp.concatenate(bots, axis=0), jnp.concatenate([dyh, dyh], axis=0))
        low = low_lane[:half]
        dx_ref[:half, lanes] = jnp.where(low, top[:half], top[half:])
        dx_ref[half:, lanes] = jnp.where(low, bot[:half], bot[half:])
    hi, lo = split2(jnp.where(ok, wt[...], 0.0))
    wb_ref[...] = mm(hi, cc) + mm(lo, cc)
    wc_ref[...] = mm(hi, bb, TN) + mm(lo, bb, TN)
    upper = tri(lambda r, a: r < a)
    rows_ref[...] = sum(mm(v, upper) for v in split3(rows_s[...]))


def enter_kernel(head0, chained, *refs):
    refs = list(refs)
    x_ref, dy_ref, b_ref, c_ref, fsb_ref, teb_ref, edge_ref, e_ref, st_ref, co_ref, dxl_ref, wb, wc, rows_ref = refs[:14]
    refs = refs[14:]
    if chained:
        pgb, pgc = refs[:2]
        refs = refs[4:]
    dx_ref, gb_ref, gc_ref, gl_ref, oh2, pick, edges = refs
    b = pl.program_id(0)
    cols = x_ref.shape[1]
    hg = gl_ref.shape[0]

    @pl.when(b == 0)
    def _():
        oh2[...] = expander(head0, cols)
        pick[...] = collector(cols)
        edges[...] = mm(side_by_side(edge_ref[...]), oh2[...])

    fcat = side_by_side(fsb_ref[...])
    tcat = side_by_side(teb_ref[...])
    bcat = jnp.concatenate([b_ref[...]] * 2, axis=1)
    ccat = jnp.concatenate([c_ref[...]] * 2, axis=1)
    gb = wb[...]
    gc = wc[...]
    if chained:
        gb = gb + pgb[...]
        gc = gc + pgc[...]
    col = jnp.zeros((BLOCK, LANES), F32)
    later = jnp.zeros((BLOCK, LANES), F32)
    end_row = iota2((8, TILE), 0) == 7
    for i in range(cols // TILE):
        lanes = slice(i * TILE, (i + 1) * TILE)
        te = mm(tcat, oh2[:, lanes])
        fs = mm(fcat, oh2[:, lanes])
        state = st_ref[0, :, lanes] + edges[pl.ds(b, 1), lanes] * e_ref[:N, lanes]
        costate = co_ref[0, :, lanes] + edges[pl.ds(8 + b, 1), lanes] * e_ref[N:, lanes]
        joined = fs[BLOCK - 1 :] * jnp.sum(state * costate, axis=0, keepdims=True)
        sst = stack2(state)
        gst = stack2(costate)
        x = x_ref[:, lanes].astype(F32)
        xs = x * te
        dys = dy_ref[:, lanes].astype(F32) * fs
        dx = dxl_ref[:, lanes] + te * mm(bcat, gst)
        dx_ref[:, lanes] = dx.astype(BF16)
        read = dys * mm(ccat, sst)
        read = jnp.concatenate([read[:-8], read[-8:] + jnp.where(end_row, joined, 0.0)], axis=0)
        col = col + collect(x * dx, pick[lanes, :])
        later = later + collect(read, pick[lanes, :])
        gc = gc + contract_states(dys, sst)
        gb = gb + contract_states(xs, gst)
    gb_ref[...] = gb
    gc_ref[...] = gc
    before = tri(lambda a, r: r < a)
    onward = tri(lambda a, r: r >= a)
    glt = sum(mm(before, v) for v in split3(col)) + sum(mm(onward, v) for v in split3(later))
    gl_ref[...] = jnp.transpose(glt)[:hg] - rows_ref[...]


def params():
    return pltpu.CompilerParams(vmem_limit_bytes=58 * 1024 * 1024)


SMEM = functools.partial(pl.BlockSpec, memory_space=pltpu.SMEM)
ANY = functools.partial(pl.BlockSpec, memory_space=pl.ANY)


def run_prep(lf, bounds, off):
    hl, tok = lf.shape
    shapes = [(tok, LANES), (hl, tok), (tok, LANES), (tok, LANES), (16, LANES)]
    vmem = pl.BlockSpec(memory_space=pltpu.VMEM)
    return pl.pallas_call(
        functools.partial(prep_kernel, tok // BLOCK, bounds.shape[0]),
        out_shape=[jax.ShapeDtypeStruct(s, F32) for s in shapes],
        in_specs=[SMEM(), SMEM(), vmem],
        out_specs=[vmem] * 5,
        compiler_params=params(),
        cost_estimate=pl.CostEstimate(flops=10**8, bytes_accessed=4 * 10**6, transcendentals=0),
        name="prep",
    )(bounds, off, lf)


def run_summary(g, cols, x, dy, b, c, fsb, teb):
    tok = x.shape[0]
    nb = tok // BLOCK
    t0 = g * cols // TILE
    tall = pl.BlockSpec((tok, TILE), lambda j: (0, t0 + j))
    full = pl.BlockSpec((tok, LANES), lambda j: (0, 0))
    blocks = pl.BlockSpec((nb, N, TILE), lambda j: (0, 0, j))
    return pl.pallas_call(
        functools.partial(summary_kernel, nb, g * cols // P_SIZE),
        grid=(cols // TILE,),
        out_shape=[
            jax.ShapeDtypeStruct((2 * N + 8, cols), F32),
            jax.ShapeDtypeStruct((nb, N, cols), F32),
            jax.ShapeDtypeStruct((nb, N, cols), F32),
        ],
        in_specs=[tall, tall, full, full, full, full],
        out_specs=[pl.BlockSpec((2 * N + 8, TILE), lambda j: (0, j)), blocks, blocks],
        compiler_params=params(),
        cost_estimate=pl.CostEstimate(flops=8 * tok * N * cols, bytes_accessed=tok * cols * 12, transcendentals=0),
        name="summary",
    )(x, dy, b, c, fsb, teb)


def run_local(g, blk0, count, cols, x, dy, b, c, cumt, cumr, bounds, off, carry):
    tok = x.shape[0]
    hg = cols // P_SIZE
    piece = pl.BlockSpec((BLOCK, cols), lambda i: (blk0 + i, g))
    thin = pl.BlockSpec((BLOCK, LANES), lambda i: (blk0 + i, 0))
    in_specs = [SMEM(), SMEM(), piece, piece, thin, thin, thin, pl.BlockSpec((hg, BLOCK), lambda i: (g, blk0 + i))]
    operands = [bounds, off, x, dy, b, c, cumt, cumr]
    aliases = {}
    if carry is not None:
        in_specs += [ANY()] * 4
        aliases = {8 + i: i for i in range(4)}
        operands += list(carry)
    return pl.pallas_call(
        functools.partial(local_kernel, blk0, g * hg, bounds.shape[0], carry is not None),
        grid=(count,),
        out_shape=[
            jax.ShapeDtypeStruct((tok, cols), F32),
            jax.ShapeDtypeStruct((tok, N), F32),
            jax.ShapeDtypeStruct((tok, N), F32),
            jax.ShapeDtypeStruct((hg, tok), F32),
        ],
        in_specs=in_specs,
        out_specs=[
            pl.BlockSpec((BLOCK, cols), lambda i: (blk0 + i, 0)),
            thin,
            thin,
            pl.BlockSpec((hg, BLOCK), lambda i: (0, blk0 + i)),
        ],
        scratch_shapes=[
            pltpu.VMEM((BLOCK, BLOCK), F32),
            pltpu.VMEM((BLOCK, BLOCK), F32),
            pltpu.VMEM((hg, BLOCK), F32),
        ],
        input_output_aliases=aliases,
        compiler_params=params(),
        cost_estimate=pl.CostEstimate(
            flops=16 * BLOCK * BLOCK * cols * count, bytes_accessed=BLOCK * cols * 8 * count, transcendentals=0
        ),
        name="local",
    )(*operands)


def run_enter(g, cols, x, dy, b, c, fsb, teb, edge, e, st, co, dxl, wb, wc, rows, carry):
    tok, wide = x.shape
    hg = cols // P_SIZE
    piece = pl.BlockSpec((BLOCK, cols), lambda i: (i, g))
    thin = pl.BlockSpec((BLOCK, LANES), lambda i: (i, 0))
    state = pl.BlockSpec((1, N, cols), lambda i: (i, 0, 0))
    in_specs = [piece, piece, thin, thin, thin, thin]
    in_specs += [pl.BlockSpec((16, LANES), lambda i: (0, 0)), pl.BlockSpec((2 * N, cols), lambda i: (0, 0))]
    in_specs += [state, state, pl.BlockSpec((BLOCK, cols), lambda i: (i, 0)), thin, thin]
    in_specs.append(pl.BlockSpec((hg, BLOCK), lambda i: (0, i)))
    operands = [x, dy, b, c, fsb, teb, edge, e, st, co, dxl, wb, wc, rows]
    aliases = {}
    if carry is not None:
        dx, gb, gc, gl = carry
        aliases = {14: 1, 15: 2, 16: 0, 17: 3}
        in_specs += [thin, thin, ANY(), ANY()]
        operands += [gb, gc, dx, gl]
    return pl.pallas_call(
        functools.partial(enter_kernel, g * hg, carry is not None),
        grid=(tok // BLOCK,),
        out_shape=[
            jax.ShapeDtypeStruct((tok, wide), BF16),
            jax.ShapeDtypeStruct((tok, N), F32),
            jax.ShapeDtypeStruct((tok, N), F32),
            jax.ShapeDtypeStruct((wide // P_SIZE, tok), F32),
        ],
        in_specs=in_specs,
        out_specs=[piece, thin, thin, pl.BlockSpec((hg, BLOCK), lambda i: (g, i))],
        scratch_shapes=[
            pltpu.VMEM((2 * LANES, cols), BF16),
            pltpu.VMEM((cols, LANES), BF16),
            pltpu.VMEM((16, cols), F32),
        ],
        input_output_aliases=aliases,
        compiler_params=params(),
        cost_estimate=pl.CostEstimate(flops=20 * tok * N * cols, bytes_accessed=tok * cols * 12, transcendentals=0),
        name="enter",
    )(*operands)


def pick_by(index, options):
    out = options[0]
    for i in range(1, len(options)):
        out = jnp.where(index == i, options[i], out)
    return out


def parts_of(pay):
    return pay[:N], pay[N : 2 * N], pay[2 * N : 2 * N + 1]


def scan_over_seq(pay, n_seq, me):
    mid_n = n_seq // (2 * OUTER)
    core = me % 2
    mid = (me // 2) % mid_n
    cols = pay.shape[1]
    half = cols // 2
    w = half // mid_n

    def at(i):
        return i // (2 * mid_n), (i // 2) % mid_n, i % 2

    def index(o, m, c):
        return (o * mid_n + m) * 2 + c

    every = range(n_seq)
    swap = [(i, i ^ 1) for i in every]

    def mid_perm(s):
        return [(i, index(at(i)[0], (at(i)[1] + s) % mid_n, at(i)[2])) for i in every]

    def outer_perm(s):
        return [(i, (i + s * 2 * mid_n) % n_seq) for i in every]

    mine = lax.dynamic_slice_in_dim(pay, core * half, half, 1)
    theirs = lax.dynamic_slice_in_dim(pay, (1 - core) * half, half, 1)
    (got,) = yield [(theirs, swap)]
    f0, b0, d0 = parts_of(jnp.where(core == 0, mine, got))
    f1, b1, d1 = parts_of(jnp.where(core == 0, got, mine))
    chip = jnp.concatenate([d1 * f0 + f1, b0 + d0 * b1, jnp.broadcast_to(d0 * d1, (8, half))], axis=0)

    slices = [chip[:, q * w : (q + 1) * w] for q in range(mid_n)]
    own = pick_by(mid, slices)
    got = yield [(pick_by((mid + s) % mid_n, slices), mid_perm(s)) for s in range(1, mid_n)]
    recv = [own] + got
    chips = [parts_of(pick_by((mid - q) % mid_n, recv)) for q in range(mid_n)]
    pf, pb, pd = chips[0]
    for f, b, d in chips[1:]:
        pf, pb, pd = d * pf + f, pb + pd * b, pd * d
    outer = me // (2 * mid_n)
    pd8 = jnp.broadcast_to(pd, (8, w))
    sends = []
    for s in range(1, OUTER):
        up = outer + s < OUTER
        sends.append((jnp.concatenate([jnp.where(up, pf, pb), pd8], axis=0), outer_perm(s)))
    got = yield sends

    def fold(arrived, reach):
        acc = jnp.zeros((N, w), F32)
        for s in range(OUTER - 1, 0, -1):
            v = arrived[s - 1]
            acc = jnp.where(s <= reach, v[:N] + v[N : N + 1] * acc, 0.0)
        return acc

    ef = fold(got, outer)
    eb = fold(got[::-1], OUTER - 1 - outer)
    enter_f = []
    for f, b, d in chips:
        enter_f.append(ef)
        ef = d * ef + f
    enter_b = []
    for f, b, d in chips[::-1]:
        enter_b.append(eb)
        eb = b + d * eb
    enters = [jnp.concatenate(v, axis=0) for v in zip(enter_f, enter_b[::-1])]
    got = yield [(pick_by((mid + s) % mid_n, enters), mid_perm(s)) for s in range(1, mid_n)]
    back = [pick_by(mid, enters)] + got
    chip_e = jnp.concatenate([pick_by((mid - q) % mid_n, back) for q in range(mid_n)], axis=1)
    cf, cb = chip_e[:N], chip_e[N:]
    first = jnp.concatenate([cf, b1 + d1 * cb], axis=0)
    second = jnp.concatenate([f0 + d0 * cf, cb], axis=0)
    keep = jnp.where(core == 0, first, second)
    (got,) = yield [(jnp.where(core == 0, second, first), swap)]
    yield jnp.concatenate([jnp.where(core == 0, keep, got), jnp.where(core == 0, got, keep)], axis=1)


def sum_over_head(parts, n_head):
    me = lax.axis_index("head")
    cut = [v.reshape(n_head, -1, v.shape[1]) for v in parts]

    def piece(k):
        return jnp.concatenate([lax.dynamic_index_in_dim(v, k, 0, keepdims=False) for v in cut], axis=0)

    total = piece(me)
    for s in range(1, n_head):
        perm = [(i, (i + s) % n_head) for i in range(n_head)]
        total = total + lax.ppermute(piece((me + s) % n_head), "head", perm)
    rows = total.shape[0] // len(parts)
    return [total[i * rows : (i + 1) * rows] for i in range(len(parts))]


def on_device(n_seq, n_head, x, dy, b, c, lf, bounds):
    tok, wide = x.shape
    hl = lf.shape[0]
    nb = tok // BLOCK
    me = lax.axis_index("seq")
    off = (me * tok).astype(jnp.int32).reshape(1)
    groups = 2 if wide // 2 >= n_seq // OUTER * LANES else 1
    cols = wide // groups
    cumt, cumr, fsb, teb, edge = run_prep(lf, bounds, off)
    sums = [None] * groups
    scans = [None] * groups
    enters = [None] * groups
    sends = [None] * groups
    done = [0] * groups
    parts = [None] * groups
    gate = cumr
    out = None

    def summarise(g):
        summed = run_summary(g, cols, x, dy, b, c, fsb, teb)
        sums[g] = summed[1:]
        scans[g] = scan_over_seq(summed[0], n_seq, me)
        sends[g] = next(scans[g])

    def local(g, count):
        parts[g] = run_local(g, done[g], count, cols, x, dy, b, c, cumt, gate, bounds, off, parts[g])
        done[g] += count

    def enter(g):
        nonlocal out
        out = run_enter(g, cols, x, dy, b, c, fsb, teb, edge, enters[g], *sums[g], *parts[g], out)

    def fly(moving):
        return [[lax.ppermute(v, "seq", p) for v, p in sends[g]] for g in moving]

    def land(moving, arrived):
        nonlocal gate, parts, out
        arrived, gate, parts, out = lax.optimization_barrier((arrived, gate, parts, out))
        for g, got in zip(moving, arrived):
            nxt = scans[g].send(got)
            if isinstance(nxt, list):
                sends[g] = nxt
            else:
                enters[g] = nxt

    summarise(0)
    if groups == 1:
        plan = [([0], [(0, 1)]), ([0], [(0, 1)]), ([0], [(0, nb - 2)]), ([0], []), ([0], [])]
    else:
        arrived = fly([0])
        summarise(1)
        land([0], arrived)
        plan = [
            ([0, 1], [(0, 1)]),
            ([0, 1], [(0, nb - 1)]),
            ([0, 1], [(1, nb - 1)]),
            ([0, 1], [(1, 1)]),
            ([1], [(0, 0)]),
        ]
    for moving, work in plan:
        arrived = fly(moving)
        for g, count in work:
            if count:
                local(g, count)
            else:
                enter(g)
        land(moving, arrived)
    enter(groups - 1)
    dx, gb, gc, gl = out
    out_b, out_c = sum_over_head([gb, gc], n_head)
    return dx, out_b.astype(BF16), out_c.astype(BF16), gl


def solution(mesh):
    return jax.shard_map(
        functools.partial(on_device, mesh.shape["seq"], mesh.shape["head"]),
        mesh=mesh,
        in_specs=(
            P("seq", "head"),
            P("seq", "head"),
            P("seq", None),
            P("seq", None),
            P("head", "seq"),
            P(),
        ),
        out_specs=(
            P("seq", "head"),
            P(("seq", "head"), None),
            P(("seq", "head"), None),
            P("head", "seq"),
        ),
        check_vma=False,
    )
```

```python
import functools

import jax
import jax.numpy as jnp
from jax import lax
from jax.experimental import pallas as pl
from jax.experimental.pallas import tpu as pltpu
from jax.sharding import PartitionSpec as P

P_SIZE = 64
N = 128
BLOCK = 256
TILE = 256
HPT = TILE // P_SIZE
LANES = 128
OUTER = 4
LOG2E = 1.4426950408889634
F32 = jnp.float32
BF16 = jnp.bfloat16

NN = (((1,), (0,)), ((), ()))
NT = (((1,), (1,)), ((), ()))
TN = (((0,), (0,)), ((), ()))


def mm(a, b, dims=NN):
    return lax.dot_general(a, b, dims, preferred_element_type=F32)


def split2(v):
    hi = v.astype(BF16)
    return hi, (v - hi.astype(F32)).astype(BF16)


def split3(v):
    hi = v.astype(BF16)
    rest = v - hi.astype(F32)
    mid = rest.astype(BF16)
    return hi, mid, (rest - mid.astype(F32)).astype(BF16)


def iota2(shape, dim):
    return lax.broadcasted_iota(jnp.int32, shape, dim)


def ones_where(cond):
    return jnp.where(cond, 1.0, 0.0).astype(BF16)


def expander(first_head, cols):
    r = iota2((2 * LANES, cols), 0) & (LANES - 1)
    c = iota2((2 * LANES, cols), 1) >> 6
    return ones_where(r == c + first_head)


def collector(cols):
    c = iota2((cols, LANES), 0) >> 6
    h = iota2((cols, LANES), 1)
    return ones_where(h == c)


def side_by_side(v):
    return jnp.concatenate(split2(v), axis=1)


def stack2(v):
    return jnp.concatenate(split2(v), axis=0)


def collect(v, onehot):
    hi, lo = split2(v)
    return mm(hi, onehot) + mm(lo, onehot)


def contract_states(scaled, stacked):
    hi, lo = split2(scaled)
    both = mm(hi, stacked, NT)
    return both[:, :N] + both[:, N:] + mm(lo, stacked[:N], NT)


def tri(cond_of):
    return ones_where(cond_of(iota2((BLOCK, BLOCK), 0), iota2((BLOCK, BLOCK), 1)))


def prepare(nb, nbounds, bounds, off, lf_ref, cumt_ref, cumr_ref, fsb_ref, teb_ref, edge_ref):
    hl = lf_ref.shape[0]
    tok = nb * BLOCK
    lower = tri(lambda t, s: s <= t)
    upper = tri(lambda s, t: s <= t)
    local = [bounds[k] - off[0] for k in range(nbounds)]

    def first_from(start):
        out = tok
        for v in local:
            out = jnp.minimum(out, jnp.where(v >= start, v, tok))
        return out

    def last_before(end):
        out = -1
        for v in local:
            out = jnp.maximum(out, jnp.where(v < end, v, -1))
        return out

    t_loc = iota2((BLOCK, LANES), 0)
    lasts = []
    for b in range(nb):
        rows = slice(b * BLOCK, (b + 1) * BLOCK)
        lf_pad = jnp.concatenate([lf_ref[:, rows], jnp.zeros((LANES - hl, BLOCK), F32)], axis=0)
        parts = split3(lf_pad)
        cumt = sum(mm(lower, p, NT) for p in parts)
        cumr = sum(mm(p, upper) for p in parts)
        cumt_ref[rows, :] = cumt * LOG2E
        cumr_ref[:, rows] = cumr[:hl] * LOG2E
        last = cumt[BLOCK - 1 : BLOCK]
        lasts.append(last)
        t = t_loc + b * BLOCK
        fsb_ref[rows, :] = jnp.where(t >= first_from(b * BLOCK), 0.0, jnp.exp(cumt))
        teb_ref[rows, :] = jnp.where(
            t < last_before((b + 1) * BLOCK), 0.0, jnp.exp(jnp.minimum(last - cumt, 0.0))
        )
    zero = jnp.zeros((1, LANES), F32)
    first = first_from(0)
    final = last_before(tok)
    for b in range(8):
        if b < nb:
            into = jnp.exp(sum(lasts[:b], zero))
            outof = jnp.exp(sum(lasts[b + 1 :], zero))
            edge_ref[b : b + 1, :] = jnp.where(first >= b * BLOCK, into, 0.0)
            edge_ref[8 + b : 9 + b, :] = jnp.where(final < (b + 1) * BLOCK, outof, 0.0)
        else:
            edge_ref[b : b + 1, :] = zero
            edge_ref[8 + b : 9 + b, :] = zero


def summary_kernel(nb, head0, nbounds, preparing, base, *refs):
    x_ref, dy_ref, b_ref, c_ref = refs[:4]
    i = pl.program_id(0)
    tiles = pl.num_programs(0)
    if preparing:
        bounds, off, lf_ref = refs[4:7]
        mine_ref, theirs_ref, st_ref, co_ref, *made = refs[7:]
        fsb_ref, teb_ref = made[2:4]

        @pl.when(i == 0)
        def _():
            prepare(nb, nbounds, bounds, off, lf_ref, *made)

    else:
        fsb_ref, teb_ref, mine_ref, theirs_ref, st_ref, co_ref = refs[4:]
    oh2 = expander(head0 + lax.rem(base[0] + i, tiles) * HPT, TILE)
    state = jnp.zeros((N, TILE), F32)
    costate = jnp.zeros((N, TILE), F32)
    whole = jnp.ones((1, TILE), F32)
    tots = [
        mm(side_by_side(fsb_ref[(b + 1) * BLOCK - 8 : (b + 1) * BLOCK, :]), oh2)[7:8] for b in range(nb)
    ]
    for b in range(nb):
        rows = slice(b * BLOCK, (b + 1) * BLOCK)
        st_ref[b] = state
        te = mm(side_by_side(teb_ref[rows, :]), oh2)
        hi, lo = split2(x_ref[rows, :].astype(F32) * te)
        bb = b_ref[rows, :]
        state = tots[b] * state + (mm(bb, hi, TN) + mm(bb, lo, TN))
        r = nb - 1 - b
        rows = slice(r * BLOCK, (r + 1) * BLOCK)
        co_ref[r] = costate
        fs = mm(side_by_side(fsb_ref[rows, :]), oh2)
        hi, lo = split2(dy_ref[rows, :].astype(F32) * fs)
        cc = c_ref[rows, :]
        costate = tots[r] * costate + (mm(cc, hi, TN) + mm(cc, lo, TN))
        whole = whole * tots[b]

    def put(ref):
        ref[0:N] = state
        ref[N : 2 * N] = costate
        ref[2 * N : 2 * N + 8] = jnp.broadcast_to(whole, (8, TILE))

    @pl.when(i < tiles // 2)
    def _():
        put(theirs_ref)

    @pl.when(i >= tiles // 2)
    def _():
        put(mine_ref)


def local_kernel(blk0, head0, nbounds, chained, *refs):
    refs = list(refs)
    bounds, off, x_ref, dy_ref, b_ref, c_ref, cumt_ref, cumr_ref = refs[:8]
    dx_ref, wb_ref, wc_ref, rows_ref, gt, wt, rows_s = refs[12:] if chained else refs[8:]
    start = off[0] + (blk0 + pl.program_id(0)) * BLOCK
    half = BLOCK // 2
    pairs = x_ref.shape[1] // LANES

    def segments(shape, dim):
        pos = iota2(shape, dim) + start
        seg = jnp.zeros(shape, jnp.int32)
        for k in range(nbounds):
            seg = seg + jnp.where(pos >= bounds[k], 1, 0)
        return seg

    ok = (segments((BLOCK, 1), 0) == segments((1, BLOCK), 1)) & (
        iota2((BLOCK, BLOCK), 0) <= iota2((BLOCK, BLOCK), 1)
    )
    bb = b_ref[...]
    cc = c_ref[...]
    gt[...] = jnp.where(ok, mm(bb, cc, NT), 0.0)
    wt[...] = jnp.zeros_like(wt)
    low_lane = iota2((BLOCK, LANES), 1) < P_SIZE
    for p in range(pairs):
        lanes = slice(p * LANES, (p + 1) * LANES)
        xp = x_ref[:, lanes]
        dyp = dy_ref[:, lanes]
        none = jnp.zeros_like(xp)
        picked = jnp.concatenate([jnp.where(low_lane, xp, none), jnp.where(low_lane, none, xp)], axis=0)
        prod = mm(picked, dyp, NT)
        tops = []
        bots = []
        acc = None
        for q in range(2):
            k = 2 * p + q
            pq = prod[q * BLOCK : (q + 1) * BLOCK]
            cr = cumr_ref[k : k + 1, :]
            cb = jnp.broadcast_to(cumt_ref[:, head0 + k : head0 + k + 1], (BLOCK, half))
            d00 = jnp.exp2(jnp.minimum(cr[:, :half] - cb[:half], 0.0))
            d01 = jnp.exp2(cr[:, half:] - cb[:half])
            d11 = jnp.exp2(jnp.minimum(cr[:, half:] - cb[half:], 0.0))
            a00 = pq[:half, :half] * d00
            a01 = pq[:half, half:] * d01
            a11 = pq[half:, half:] * d11
            acc = (a00, a01, a11) if q == 0 else (acc[0] + a00, acc[1] + a01, acc[2] + a11)
            g00 = gt[:half, :half]
            g01 = gt[:half, half:]
            g11 = gt[half:, half:]
            rows_s[k : k + 1, :half] = jnp.sum(a00 * g00, axis=0, keepdims=True)
            rows_s[k : k + 1, half:] = jnp.sum(a01 * g01 + a11 * g11, axis=0, keepdims=True)
            h00, l00 = split2(d00 * g00)
            h01, l01 = split2(d01 * g01)
            h11, l11 = split2(d11 * g11)
            tops.append(jnp.concatenate([h00, h01, l00, l01], axis=1))
            bots.append(jnp.concatenate([h11, l11], axis=1))
        wt[:half, :half] += acc[0]
        wt[:half, half:] += acc[1]
        wt[half:, half:] += acc[2]
        dyh = dyp[half:]
        top = mm(jnp.concatenate(tops, axis=0), jnp.concatenate([dyp, dyp], axis=0))
        bot = mm(jnp.concatenate(bots, axis=0), jnp.concatenate([dyh, dyh], axis=0))
        low = low_lane[:half]
        dx_ref[:half, lanes] = jnp.where(low, top[:half], top[half:])
        dx_ref[half:, lanes] = jnp.where(low, bot[:half], bot[half:])
    hi, lo = split2(jnp.where(ok, wt[...], 0.0))
    wb_ref[...] = mm(hi, cc) + mm(lo, cc)
    wc_ref[...] = mm(hi, bb, TN) + mm(lo, bb, TN)
    upper = tri(lambda r, a: r < a)
    rows_ref[...] = sum(mm(v, upper) for v in split3(rows_s[...]))


def enter_kernel(nb, head0, adding, aliased, *refs):
    refs = list(refs)
    order = refs[0]
    x_ref, dy_ref, b_ref, c_ref, fsb_ref, teb_ref, edge_ref, ek_ref, eg_ref, st_ref, co_ref, dxl_ref, wb, wc, rows_ref = refs[1:16]
    refs = refs[16:]
    if adding:
        pgb, pgc = refs[:2]
        refs = refs[2:]
    if aliased:
        refs = refs[2:]
    dx_ref, gb_ref, gc_ref, gl_ref, oh2, pick, edges = refs
    b = lax.rem(order[0] + pl.program_id(0), nb)
    cols = x_ref.shape[1]
    hg = gl_ref.shape[0]

    @pl.when(pl.program_id(0) == 0)
    def _():
        oh2[...] = expander(head0, cols)
        pick[...] = collector(cols)
        edges[...] = mm(side_by_side(edge_ref[...]), oh2[...])

    fcat = side_by_side(fsb_ref[...])
    tcat = side_by_side(teb_ref[...])
    bcat = jnp.concatenate([b_ref[...]] * 2, axis=1)
    ccat = jnp.concatenate([c_ref[...]] * 2, axis=1)
    gb = wb[...]
    gc = wc[...]
    if adding:
        gb = gb + pgb[...]
        gc = gc + pgc[...]
    col = jnp.zeros((BLOCK, LANES), F32)
    later = jnp.zeros((BLOCK, LANES), F32)
    end_row = iota2((8, TILE), 0) == 7
    for i in range(cols // TILE):
        side, begin = divmod(i * TILE, cols // 2)
        lanes = pl.ds(pl.multiple_of(lax.rem(order[1] + side, 2) * (cols // 2) + begin, TILE), TILE)
        te = mm(tcat, oh2[:, lanes])
        fs = mm(fcat, oh2[:, lanes])
        e = (eg_ref if side else ek_ref)[:, begin : begin + TILE]
        state = st_ref[0, :, lanes] + edges[pl.ds(b, 1), lanes] * e[:N]
        costate = co_ref[0, :, lanes] + edges[pl.ds(8 + b, 1), lanes] * e[N:]
        joined = fs[BLOCK - 1 :] * jnp.sum(state * costate, axis=0, keepdims=True)
        sst = stack2(state)
        gst = stack2(costate)
        x = x_ref[:, lanes].astype(F32)
        xs = x * te
        dys = dy_ref[:, lanes].astype(F32) * fs
        dx = dxl_ref[:, lanes] + te * mm(bcat, gst)
        dx_ref[:, lanes] = dx.astype(BF16)
        read = dys * mm(ccat, sst)
        read = jnp.concatenate([read[:-8], read[-8:] + jnp.where(end_row, joined, 0.0)], axis=0)
        col = col + collect(x * dx, pick[lanes, :])
        later = later + collect(read, pick[lanes, :])
        gc = gc + contract_states(dys, sst)
        gb = gb + contract_states(xs, gst)
    gb_ref[...] = gb
    gc_ref[...] = gc
    before = tri(lambda a, r: r < a)
    onward = tri(lambda a, r: r >= a)
    glt = sum(mm(before, v) for v in split3(col)) + sum(mm(onward, v) for v in split3(later))
    gl_ref[...] = jnp.transpose(glt)[:hg] - rows_ref[...]


def params():
    return pltpu.CompilerParams(vmem_limit_bytes=58 * 1024 * 1024)


SMEM = functools.partial(pl.BlockSpec, memory_space=pltpu.SMEM)
ANY = functools.partial(pl.BlockSpec, memory_space=pl.ANY)


def run_summary(g, cols, core, x, dy, b, c, made):
    tok = x.shape[0]
    nb = tok // BLOCK
    tiles = cols // TILE
    t0 = g * tiles
    base = ((1 - core) * (tiles // 2)).astype(jnp.int32).reshape(1)

    def spec(shape, place):
        return pl.BlockSpec(shape, lambda i, o: place(i, lax.rem(o[0] + i, tiles)))

    tall = spec((tok, TILE), lambda i, j: (0, t0 + j))
    full = spec((tok, LANES), lambda i, j: (0, 0))
    blocks = spec((nb, N, TILE), lambda i, j: (0, 0, j))
    in_specs = [tall, tall, full, full]
    operands = [base, x, dy, b, c]
    half = (2 * N + 8, cols // 2)
    shapes = [half, half, (nb, N, cols), (nb, N, cols)]
    out_specs = [
        spec((2 * N + 8, TILE), lambda i, j: (0, jnp.maximum(i - tiles // 2, 0))),
        spec((2 * N + 8, TILE), lambda i, j: (0, jnp.minimum(i, tiles // 2 - 1))),
        blocks,
        blocks,
    ]
    preparing = len(made) == 3
    nbounds = 0
    if preparing:
        bounds, off, lf = made
        nbounds = bounds.shape[0]
        hl = lf.shape[0]
        in_specs += [SMEM(), SMEM(), spec((hl, tok), lambda i, j: (0, 0))]
        extra = [(tok, LANES), (hl, tok), (tok, LANES), (tok, LANES), (16, LANES)]
        shapes += extra
        out_specs += [spec(v, lambda i, j: (0, 0)) for v in extra]
        operands += [bounds, off, lf]
    else:
        in_specs += [full, full]
        operands += [made[2], made[3]]
    out = pl.pallas_call(
        functools.partial(summary_kernel, nb, g * cols // P_SIZE, nbounds, preparing),
        grid_spec=pltpu.PrefetchScalarGridSpec(
            num_scalar_prefetch=1, grid=(tiles,), in_specs=in_specs, out_specs=out_specs
        ),
        out_shape=[jax.ShapeDtypeStruct(v, F32) for v in shapes],
        compiler_params=params(),
        cost_estimate=pl.CostEstimate(flops=8 * tok * N * cols, bytes_accessed=tok * cols * 12, transcendentals=0),
        name="summary",
    )(*operands)
    return out[:2], out[2:4], out[4:] if preparing else made


def run_local(g, blk0, count, cols, x, dy, b, c, cumt, cumr, bounds, off, carry):
    tok = x.shape[0]
    hg = cols // P_SIZE
    piece = pl.BlockSpec((BLOCK, cols), lambda i: (blk0 + i, g))
    thin = pl.BlockSpec((BLOCK, LANES), lambda i: (blk0 + i, 0))
    in_specs = [SMEM(), SMEM(), piece, piece, thin, thin, thin, pl.BlockSpec((hg, BLOCK), lambda i: (g, blk0 + i))]
    operands = [bounds, off, x, dy, b, c, cumt, cumr]
    aliases = {}
    if carry is not None:
        in_specs += [ANY()] * 4
        aliases = {8 + i: i for i in range(4)}
        operands += list(carry)
    return pl.pallas_call(
        functools.partial(local_kernel, blk0, g * hg, bounds.shape[0], carry is not None),
        grid=(count,),
        out_shape=[
            jax.ShapeDtypeStruct((tok, cols), F32),
            jax.ShapeDtypeStruct((tok, N), F32),
            jax.ShapeDtypeStruct((tok, N), F32),
            jax.ShapeDtypeStruct((hg, tok), F32),
        ],
        in_specs=in_specs,
        out_specs=[
            pl.BlockSpec((BLOCK, cols), lambda i: (blk0 + i, 0)),
            thin,
            thin,
            pl.BlockSpec((hg, BLOCK), lambda i: (0, blk0 + i)),
        ],
        scratch_shapes=[
            pltpu.VMEM((BLOCK, BLOCK), F32),
            pltpu.VMEM((BLOCK, BLOCK), F32),
            pltpu.VMEM((hg, BLOCK), F32),
        ],
        input_output_aliases=aliases,
        compiler_params=params(),
        cost_estimate=pl.CostEstimate(
            flops=16 * BLOCK * BLOCK * cols * count, bytes_accessed=BLOCK * cols * 8 * count, transcendentals=0
        ),
        name="local",
    )(*operands)


def run_enter(g, cols, order, count, x, dy, b, c, fsb, teb, edge, keep, got, st, co, dxl, wb, wc, rows, grads, whole):
    tok, wide = x.shape
    nb = tok // BLOCK
    hg = cols // P_SIZE

    def spec(shape, place):
        return pl.BlockSpec(shape, lambda i, o: place(lax.rem(o[0] + i, nb)))

    piece = spec((BLOCK, cols), lambda k: (k, g))
    thin = spec((BLOCK, LANES), lambda k: (k, 0))
    state = spec((1, N, cols), lambda k: (k, 0, 0))
    in_specs = [piece, piece, thin, thin, thin, thin]
    in_specs.append(spec((16, LANES), lambda k: (0, 0)))
    in_specs += [spec((2 * N, cols // 2), lambda k: (0, 0))] * 2
    in_specs += [state, state, spec((BLOCK, cols), lambda k: (k, 0)), thin, thin]
    in_specs.append(spec((hg, BLOCK), lambda k: (0, k)))
    operands = [order, x, dy, b, c, fsb, teb, edge, keep, got, st, co, dxl, wb, wc, rows]
    aliases = {}
    if grads is not None:
        aliases = {16: 1, 17: 2}
        in_specs += [thin, thin]
        operands += list(grads)
    if whole is not None:
        aliases[len(operands)] = 0
        aliases[len(operands) + 1] = 3
        in_specs += [ANY(), ANY()]
        operands += list(whole)
    dx, gb, gc, gl = pl.pallas_call(
        functools.partial(enter_kernel, nb, g * hg, grads is not None, whole is not None),
        grid_spec=pltpu.PrefetchScalarGridSpec(
            num_scalar_prefetch=1,
            grid=(count,),
            in_specs=in_specs,
            out_specs=[piece, thin, thin, spec((hg, BLOCK), lambda k: (g, k))],
            scratch_shapes=[
                pltpu.VMEM((2 * LANES, cols), BF16),
                pltpu.VMEM((cols, LANES), BF16),
                pltpu.VMEM((16, cols), F32),
            ],
        ),
        out_shape=[
            jax.ShapeDtypeStruct((tok, wide), BF16),
            jax.ShapeDtypeStruct((tok, N), F32),
            jax.ShapeDtypeStruct((tok, N), F32),
            jax.ShapeDtypeStruct((wide // P_SIZE, tok), F32),
        ],
        input_output_aliases=aliases,
        compiler_params=params(),
        cost_estimate=pl.CostEstimate(
            flops=20 * BLOCK * count * N * cols, bytes_accessed=BLOCK * count * cols * 12, transcendentals=0
        ),
        name="enter",
    )(*operands)
    return (gb, gc), (dx, gl)


def pick_by(index, options):
    out = options[0]
    for i in range(1, len(options)):
        out = jnp.where(index == i, options[i], out)
    return out


def parts_of(pay):
    return pay[:N], pay[N : 2 * N], pay[2 * N : 2 * N + 1]


def scan_over_seq(mine, theirs, n_seq, me):
    mid_n = n_seq // (2 * OUTER)
    core = me % 2
    mid = (me // 2) % mid_n
    half = mine.shape[1]
    w = half // mid_n

    def at(i):
        return i // (2 * mid_n), (i // 2) % mid_n, i % 2

    def index(o, m, c):
        return (o * mid_n + m) * 2 + c

    every = range(n_seq)
    swap = [(i, i ^ 1) for i in every]

    def mid_perm(s):
        return [(i, index(at(i)[0], (at(i)[1] + s) % mid_n, at(i)[2])) for i in every]

    def outer_perm(s):
        return [(i, (i + s * 2 * mid_n) % n_seq) for i in every]

    (got,) = yield [(theirs, swap)]
    f0, b0, d0 = parts_of(jnp.where(core == 0, mine, got))
    f1, b1, d1 = parts_of(jnp.where(core == 0, got, mine))
    chip = jnp.concatenate([d1 * f0 + f1, b0 + d0 * b1, jnp.broadcast_to(d0 * d1, (8, half))], axis=0)

    slices = [chip[:, q * w : (q + 1) * w] for q in range(mid_n)]
    own = pick_by(mid, slices)
    got = yield [(pick_by((mid + s) % mid_n, slices), mid_perm(s)) for s in range(1, mid_n)]
    recv = [own] + got
    chips = [parts_of(pick_by((mid - q) % mid_n, recv)) for q in range(mid_n)]
    pf, pb, pd = chips[0]
    for f, b, d in chips[1:]:
        pf, pb, pd = d * pf + f, pb + pd * b, pd * d
    outer = me // (2 * mid_n)
    pd8 = jnp.broadcast_to(pd, (8, w))
    sends = []
    for s in range(1, OUTER):
        up = outer + s < OUTER
        sends.append((jnp.concatenate([jnp.where(up, pf, pb), pd8], axis=0), outer_perm(s)))
    got = yield sends

    def fold(arrived, reach):
        acc = jnp.zeros((N, w), F32)
        for s in range(OUTER - 1, 0, -1):
            v = arrived[s - 1]
            acc = jnp.where(s <= reach, v[:N] + v[N : N + 1] * acc, 0.0)
        return acc

    ef = fold(got, outer)
    eb = fold(got[::-1], OUTER - 1 - outer)
    enter_f = []
    for f, b, d in chips:
        enter_f.append(ef)
        ef = d * ef + f
    enter_b = []
    for f, b, d in chips[::-1]:
        enter_b.append(eb)
        eb = b + d * eb
    enters = [jnp.concatenate(v, axis=0) for v in zip(enter_f, enter_b[::-1])]
    got = yield [(pick_by((mid + s) % mid_n, enters), mid_perm(s)) for s in range(1, mid_n)]
    back = [pick_by(mid, enters)] + got
    chip_e = jnp.concatenate([pick_by((mid - q) % mid_n, back) for q in range(mid_n)], axis=1)
    cf, cb = chip_e[:N], chip_e[N:]
    first = jnp.concatenate([cf, b1 + d1 * cb], axis=0)
    second = jnp.concatenate([f0 + d0 * cf, cb], axis=0)
    keep = jnp.where(core == 0, first, second)
    (got,) = yield [(jnp.where(core == 0, second, first), swap)]
    yield keep, got


def shard_rows(grads, n_head, k):
    cut = [v.reshape(n_head, -1, v.shape[1]) for v in grads]
    return jnp.concatenate([lax.dynamic_index_in_dim(v, k, 0, keepdims=False) for v in cut], axis=0)


def on_device(n_seq, n_head, x, dy, b, c, lf, bounds):
    tok, wide = x.shape
    hl = lf.shape[0]
    nb = tok // BLOCK
    me = lax.axis_index("seq")
    off = (me * tok).astype(jnp.int32).reshape(1)
    groups = 2 if wide // 2 >= n_seq // OUTER * LANES else 1
    cols = wide // groups
    core = (me % 2).astype(jnp.int32)
    sums = [None] * groups
    scans = [None] * groups
    enters = [None] * groups
    sends = [None] * groups
    done = [0] * groups
    parts = [None] * groups
    made = (bounds, off, lf)
    out = None

    def summarise(g):
        nonlocal made
        halves, sums[g], made = run_summary(g, cols, core, x, dy, b, c, made)
        scans[g] = scan_over_seq(*halves, n_seq, me)
        sends[g] = next(scans[g])

    def local(g, count):
        parts[g] = run_local(g, done[g], count, cols, x, dy, b, c, cumt, gate, bounds, off, parts[g])
        done[g] += count

    me_head = lax.axis_index("head").astype(jnp.int32)
    per = nb // n_head
    others = lax.rem(me_head + 1, n_head) * per
    phases = ((jnp.stack([others, core]), nb - per), (jnp.stack([me_head * per, core]), per))
    grads = [None, None]

    def enter(g, phase):
        nonlocal out
        order, count = phases[phase]
        args = (x, dy, b, c, fsb, teb, edge, *enters[g], *sums[g], *parts[g])
        grads[phase], out = run_enter(g, cols, order, count, *args, grads[phase], out)

    def fly(moving):
        return [[lax.ppermute(v, "seq", p) for v, p in sends[g]] for g in moving]

    def land(moving, arrived):
        nonlocal gate, parts, out, grads
        arrived, gate, parts, out, grads = lax.optimization_barrier((arrived, gate, parts, out, grads))
        for g, got in zip(moving, arrived):
            nxt = scans[g].send(got)
            if isinstance(nxt, list):
                sends[g] = nxt
            else:
                enters[g] = nxt

    summarise(0)
    cumt, gate, fsb, teb, edge = made
    if groups == 1:
        plan = [([0], [(0, 1)]), ([0], [(0, 1)]), ([0], [(0, nb - 2)]), ([0], []), ([0], [])]
    else:
        arrived = fly([0])
        summarise(1)
        land([0], arrived)
        plan = [
            ([0, 1], [(0, 2)]),
            ([0, 1], [(0, nb - 2)]),
            ([0, 1], [(1, nb - 2)]),
            ([0, 1], [(1, 2)]),
            ([1], [(0, 0)]),
        ]
    for moving, work in plan:
        arrived = fly(moving)
        for g, count in work:
            if count:
                local(g, count)
            else:
                enter(g, 0)
        land(moving, arrived)
    enter(groups - 1, 0)
    away = []
    for s in range(1, n_head):
        away.append(shard_rows(grads[0], n_head, lax.rem(me_head + s, n_head)))
    away, out = lax.optimization_barrier((away, out))
    arrived = []
    for s, v in zip(range(1, n_head), away):
        arrived.append(lax.ppermute(v, "head", [(i, (i + s) % n_head) for i in range(n_head)]))
    for g in range(groups):
        enter(g, 1)
    total = shard_rows(grads[1], n_head, me_head)
    for v in arrived:
        total = total + v
    total = total.astype(BF16)
    rows = tok // n_head
    dx, gl = out
    return dx, total[:rows], total[rows:], gl


def solution(mesh):
    return jax.shard_map(
        functools.partial(on_device, mesh.shape["seq"], mesh.shape["head"]),
        mesh=mesh,
        in_specs=(
            P("seq", "head"),
            P("seq", "head"),
            P("seq", None),
            P("seq", None),
            P("head", "seq"),
            P(),
        ),
        out_specs=(
            P("seq", "head"),
            P(("seq", "head"), None),
            P(("seq", "head"), None),
            P("head", "seq"),
        ),
        check_vma=False,
    )
```

```python
import functools

import jax
import jax.numpy as jnp
from jax import lax
from jax.experimental import pallas as pl
from jax.experimental.pallas import tpu as pltpu
from jax.sharding import PartitionSpec as P

P_SIZE = 64
N = 128
BLOCK = 256
TILE = 256
HPT = TILE // P_SIZE
LANES = 128
OUTER = 4
LOG2E = 1.4426950408889634
F32 = jnp.float32
BF16 = jnp.bfloat16

NN = (((1,), (0,)), ((), ()))
NT = (((1,), (1,)), ((), ()))
TN = (((0,), (0,)), ((), ()))


def mm(a, b, dims=NN):
    return lax.dot_general(a, b, dims, preferred_element_type=F32)


def split2(v):
    hi = v.astype(BF16)
    return hi, (v - hi.astype(F32)).astype(BF16)


def split3(v):
    hi = v.astype(BF16)
    rest = v - hi.astype(F32)
    mid = rest.astype(BF16)
    return hi, mid, (rest - mid.astype(F32)).astype(BF16)


def iota2(shape, dim):
    return lax.broadcasted_iota(jnp.int32, shape, dim)


def ones_where(cond):
    return jnp.where(cond, 1.0, 0.0).astype(BF16)


def expander(first_head, cols):
    r = iota2((2 * LANES, cols), 0) & (LANES - 1)
    c = iota2((2 * LANES, cols), 1) >> 6
    return ones_where(r == c + first_head)


def collector(cols):
    c = iota2((cols, LANES), 0) >> 6
    h = iota2((cols, LANES), 1)
    return ones_where(h == c)


def side_by_side(v):
    return jnp.concatenate(split2(v), axis=1)


def stack2(v):
    return jnp.concatenate(split2(v), axis=0)


def collect(v, onehot):
    hi, lo = split2(v)
    return mm(hi, onehot) + mm(lo, onehot)


def contract_states(scaled, stacked):
    hi, lo = split2(scaled)
    both = mm(hi, stacked, NT)
    return both[:, :N] + both[:, N:] + mm(lo, stacked[:N], NT)


def tri(cond_of):
    return ones_where(cond_of(iota2((BLOCK, BLOCK), 0), iota2((BLOCK, BLOCK), 1)))


def prepare(nb, nbounds, bounds, off, lf_ref, cumt_ref, cumr_ref, fsb_ref, teb_ref, edge_ref):
    hl = lf_ref.shape[0]
    tok = nb * BLOCK
    lower = tri(lambda t, s: s <= t)
    upper = tri(lambda s, t: s <= t)
    local = [bounds[k] - off[0] for k in range(nbounds)]

    def first_from(start):
        out = tok
        for v in local:
            out = jnp.minimum(out, jnp.where(v >= start, v, tok))
        return out

    def last_before(end):
        out = -1
        for v in local:
            out = jnp.maximum(out, jnp.where(v < end, v, -1))
        return out

    t_loc = iota2((BLOCK, LANES), 0)
    lasts = []
    for b in range(nb):
        rows = slice(b * BLOCK, (b + 1) * BLOCK)
        lf_pad = jnp.concatenate([lf_ref[:, rows], jnp.zeros((LANES - hl, BLOCK), F32)], axis=0)
        parts = split3(lf_pad)
        cumt = sum(mm(lower, p, NT) for p in parts)
        cumr = sum(mm(p, upper) for p in parts)
        cumt_ref[rows, :] = cumt * LOG2E
        cumr_ref[:, rows] = cumr[:hl] * LOG2E
        last = cumt[BLOCK - 1 : BLOCK]
        lasts.append(last)
        t = t_loc + b * BLOCK
        fsb_ref[rows, :] = jnp.where(t >= first_from(b * BLOCK), 0.0, jnp.exp(cumt))
        teb_ref[rows, :] = jnp.where(
            t < last_before((b + 1) * BLOCK), 0.0, jnp.exp(jnp.minimum(last - cumt, 0.0))
        )
    zero = jnp.zeros((1, LANES), F32)
    first = first_from(0)
    final = last_before(tok)
    for b in range(8):
        if b < nb:
            into = jnp.exp(sum(lasts[:b], zero))
            outof = jnp.exp(sum(lasts[b + 1 :], zero))
            edge_ref[b : b + 1, :] = jnp.where(first >= b * BLOCK, into, 0.0)
            edge_ref[8 + b : 9 + b, :] = jnp.where(final < (b + 1) * BLOCK, outof, 0.0)
        else:
            edge_ref[b : b + 1, :] = zero
            edge_ref[8 + b : 9 + b, :] = zero


def summary_kernel(nb, head0, nbounds, preparing, base, *refs):
    x_ref, dy_ref, b_ref, c_ref = refs[:4]
    i = pl.program_id(0)
    tiles = pl.num_programs(0)
    if preparing:
        bounds, off, lf_ref = refs[4:7]
        mine_ref, theirs_ref, st_ref, co_ref, *made = refs[7:]
        fsb_ref, teb_ref = made[2:4]

        @pl.when(i == 0)
        def _():
            prepare(nb, nbounds, bounds, off, lf_ref, *made)

    else:
        fsb_ref, teb_ref, mine_ref, theirs_ref, st_ref, co_ref = refs[4:]
    oh2 = expander(head0 + lax.rem(base[0] + i, tiles) * HPT, TILE)
    state = jnp.zeros((N, TILE), F32)
    costate = jnp.zeros((N, TILE), F32)
    whole = jnp.ones((1, TILE), F32)
    tots = [
        mm(side_by_side(fsb_ref[(b + 1) * BLOCK - 8 : (b + 1) * BLOCK, :]), oh2)[7:8] for b in range(nb)
    ]
    for b in range(nb):
        rows = slice(b * BLOCK, (b + 1) * BLOCK)
        st_ref[b] = state
        te = mm(side_by_side(teb_ref[rows, :]), oh2)
        hi, lo = split2(x_ref[rows, :].astype(F32) * te)
        bb = b_ref[rows, :]
        state = tots[b] * state + (mm(bb, hi, TN) + mm(bb, lo, TN))
        r = nb - 1 - b
        rows = slice(r * BLOCK, (r + 1) * BLOCK)
        co_ref[r] = costate
        fs = mm(side_by_side(fsb_ref[rows, :]), oh2)
        hi, lo = split2(dy_ref[rows, :].astype(F32) * fs)
        cc = c_ref[rows, :]
        costate = tots[r] * costate + (mm(cc, hi, TN) + mm(cc, lo, TN))
        whole = whole * tots[b]

    def put(ref):
        ref[0:N] = state
        ref[N : 2 * N] = costate
        ref[2 * N : 2 * N + 8] = jnp.broadcast_to(whole, (8, TILE))

    @pl.when(i < tiles // 2)
    def _():
        put(theirs_ref)

    @pl.when(i >= tiles // 2)
    def _():
        put(mine_ref)


def local_kernel(blk0, head0, nbounds, chained, *refs):
    refs = list(refs)
    bounds, off, x_ref, dy_ref, b_ref, c_ref, cumt_ref, cumr_ref = refs[:8]
    dx_ref, wb_ref, wc_ref, rows_ref, gt, wt, rows_s = refs[12:] if chained else refs[8:]
    start = off[0] + (blk0 + pl.program_id(0)) * BLOCK
    half = BLOCK // 2
    pairs = x_ref.shape[1] // LANES

    def segments(shape, dim):
        pos = iota2(shape, dim) + start
        seg = jnp.zeros(shape, jnp.int32)
        for k in range(nbounds):
            seg = seg + jnp.where(pos >= bounds[k], 1, 0)
        return seg

    ok = (segments((BLOCK, 1), 0) == segments((1, BLOCK), 1)) & (
        iota2((BLOCK, BLOCK), 0) <= iota2((BLOCK, BLOCK), 1)
    )
    bb = b_ref[...]
    cc = c_ref[...]
    gt[...] = jnp.where(ok, mm(bb, cc, NT), 0.0)
    wt[...] = jnp.zeros_like(wt)
    low_lane = iota2((BLOCK, LANES), 1) < P_SIZE
    for p in range(pairs):
        lanes = slice(p * LANES, (p + 1) * LANES)
        xp = x_ref[:, lanes]
        dyp = dy_ref[:, lanes]
        none = jnp.zeros_like(xp)
        picked = jnp.concatenate([jnp.where(low_lane, xp, none), jnp.where(low_lane, none, xp)], axis=0)
        prod = mm(picked, dyp, NT)
        tops = []
        bots = []
        acc = None
        for q in range(2):
            k = 2 * p + q
            pq = prod[q * BLOCK : (q + 1) * BLOCK]
            cr = cumr_ref[k : k + 1, :]
            cb = jnp.broadcast_to(cumt_ref[:, head0 + k : head0 + k + 1], (BLOCK, half))
            d00 = jnp.exp2(jnp.minimum(cr[:, :half] - cb[:half], 0.0))
            d01 = jnp.exp2(cr[:, half:] - cb[:half])
            d11 = jnp.exp2(jnp.minimum(cr[:, half:] - cb[half:], 0.0))
            a00 = pq[:half, :half] * d00
            a01 = pq[:half, half:] * d01
            a11 = pq[half:, half:] * d11
            acc = (a00, a01, a11) if q == 0 else (acc[0] + a00, acc[1] + a01, acc[2] + a11)
            g00 = gt[:half, :half]
            g01 = gt[:half, half:]
            g11 = gt[half:, half:]
            rows_s[k : k + 1, :half] = jnp.sum(a00 * g00, axis=0, keepdims=True)
            rows_s[k : k + 1, half:] = jnp.sum(a01 * g01 + a11 * g11, axis=0, keepdims=True)
            h00, l00 = split2(d00 * g00)
            h01, l01 = split2(d01 * g01)
            h11, l11 = split2(d11 * g11)
            tops.append(jnp.concatenate([h00, h01, l00, l01], axis=1))
            bots.append(jnp.concatenate([h11, l11], axis=1))
        wt[:half, :half] += acc[0]
        wt[:half, half:] += acc[1]
        wt[half:, half:] += acc[2]
        dyh = dyp[half:]
        top = mm(jnp.concatenate(tops, axis=0), jnp.concatenate([dyp, dyp], axis=0))
        bot = mm(jnp.concatenate(bots, axis=0), jnp.concatenate([dyh, dyh], axis=0))
        low = low_lane[:half]
        dx_ref[:half, lanes] = jnp.where(low, top[:half], top[half:])
        dx_ref[half:, lanes] = jnp.where(low, bot[:half], bot[half:])
    hi, lo = split2(jnp.where(ok, wt[...], 0.0))
    wb_ref[...] = mm(hi, cc) + mm(lo, cc)
    wc_ref[...] = mm(hi, bb, TN) + mm(lo, bb, TN)
    upper = tri(lambda r, a: r < a)
    rows_ref[...] = sum(mm(v, upper) for v in split3(rows_s[...]))


def enter_kernel(nb, head0, adding, aliased, *refs):
    refs = list(refs)
    order = refs[0]
    x_ref, dy_ref, b_ref, c_ref, fsb_ref, teb_ref, edge_ref, ek_ref, eg_ref, st_ref, co_ref, dxl_ref, wb, wc, rows_ref = refs[1:16]
    refs = refs[16:]
    if adding:
        prev = refs[0]
        refs = refs[1:]
    if aliased:
        refs = refs[2:]
    dx_ref, grad_ref, gl_ref, oh2, pick, edges = refs
    b = lax.rem(order[0] + pl.program_id(0), nb)
    cols = x_ref.shape[1]
    hg = gl_ref.shape[0]

    @pl.when(pl.program_id(0) == 0)
    def _():
        oh2[...] = expander(head0, cols)
        pick[...] = collector(cols)
        edges[...] = mm(side_by_side(edge_ref[...]), oh2[...])

    fcat = side_by_side(fsb_ref[...])
    tcat = side_by_side(teb_ref[...])
    bcat = jnp.concatenate([b_ref[...]] * 2, axis=1)
    ccat = jnp.concatenate([c_ref[...]] * 2, axis=1)
    gb = wb[...]
    gc = wc[...]
    if adding:
        gb = gb + prev[0]
        gc = gc + prev[1]
    col = jnp.zeros((BLOCK, LANES), F32)
    later = jnp.zeros((BLOCK, LANES), F32)
    end_row = iota2((8, TILE), 0) == 7
    for i in range(cols // TILE):
        side, begin = divmod(i * TILE, cols // 2)
        lanes = pl.ds(pl.multiple_of(lax.rem(order[1] + side, 2) * (cols // 2) + begin, TILE), TILE)
        te = mm(tcat, oh2[:, lanes])
        fs = mm(fcat, oh2[:, lanes])
        e = (eg_ref if side else ek_ref)[:, begin : begin + TILE]
        state = st_ref[0, :, lanes] + edges[pl.ds(b, 1), lanes] * e[:N]
        costate = co_ref[0, :, lanes] + edges[pl.ds(8 + b, 1), lanes] * e[N:]
        joined = fs[BLOCK - 1 :] * jnp.sum(state * costate, axis=0, keepdims=True)
        sst = stack2(state)
        gst = stack2(costate)
        x = x_ref[:, lanes].astype(F32)
        xs = x * te
        dys = dy_ref[:, lanes].astype(F32) * fs
        dx = dxl_ref[:, lanes] + te * mm(bcat, gst)
        dx_ref[:, lanes] = dx.astype(BF16)
        read = dys * mm(ccat, sst)
        read = jnp.concatenate([read[:-8], read[-8:] + jnp.where(end_row, joined, 0.0)], axis=0)
        col = col + collect(x * dx, pick[lanes, :])
        later = later + collect(read, pick[lanes, :])
        gc = gc + contract_states(dys, sst)
        gb = gb + contract_states(xs, gst)
    grad_ref[0] = gb
    grad_ref[1] = gc
    before = tri(lambda a, r: r < a)
    onward = tri(lambda a, r: r >= a)
    glt = sum(mm(before, v) for v in split3(col)) + sum(mm(onward, v) for v in split3(later))
    gl_ref[...] = jnp.transpose(glt)[:hg] - rows_ref[...]


def params():
    return pltpu.CompilerParams(vmem_limit_bytes=58 * 1024 * 1024)


SMEM = functools.partial(pl.BlockSpec, memory_space=pltpu.SMEM)
ANY = functools.partial(pl.BlockSpec, memory_space=pl.ANY)


def run_summary(g, cols, core, x, dy, b, c, made):
    tok = x.shape[0]
    nb = tok // BLOCK
    tiles = cols // TILE
    t0 = g * tiles
    base = ((1 - core) * (tiles // 2)).astype(jnp.int32).reshape(1)

    def spec(shape, place):
        return pl.BlockSpec(shape, lambda i, o: place(i, lax.rem(o[0] + i, tiles)))

    tall = spec((tok, TILE), lambda i, j: (0, t0 + j))
    full = spec((tok, LANES), lambda i, j: (0, 0))
    blocks = spec((nb, N, TILE), lambda i, j: (0, 0, j))
    in_specs = [tall, tall, full, full]
    operands = [base, x, dy, b, c]
    half = (2 * N + 8, cols // 2)
    shapes = [half, half, (nb, N, cols), (nb, N, cols)]
    out_specs = [
        spec((2 * N + 8, TILE), lambda i, j: (0, jnp.maximum(i - tiles // 2, 0))),
        spec((2 * N + 8, TILE), lambda i, j: (0, jnp.minimum(i, tiles // 2 - 1))),
        blocks,
        blocks,
    ]
    preparing = len(made) == 3
    nbounds = 0
    if preparing:
        bounds, off, lf = made
        nbounds = bounds.shape[0]
        hl = lf.shape[0]
        in_specs += [SMEM(), SMEM(), spec((hl, tok), lambda i, j: (0, 0))]
        extra = [(tok, LANES), (hl, tok), (tok, LANES), (tok, LANES), (16, LANES)]
        shapes += extra
        out_specs += [spec(v, lambda i, j: (0, 0)) for v in extra]
        operands += [bounds, off, lf]
    else:
        in_specs += [full, full]
        operands += [made[2], made[3]]
    out = pl.pallas_call(
        functools.partial(summary_kernel, nb, g * cols // P_SIZE, nbounds, preparing),
        grid_spec=pltpu.PrefetchScalarGridSpec(
            num_scalar_prefetch=1, grid=(tiles,), in_specs=in_specs, out_specs=out_specs
        ),
        out_shape=[jax.ShapeDtypeStruct(v, F32) for v in shapes],
        compiler_params=params(),
        cost_estimate=pl.CostEstimate(flops=8 * tok * N * cols, bytes_accessed=tok * cols * 12, transcendentals=0),
        name="summary",
    )(*operands)
    return out[:2], out[2:4], out[4:] if preparing else made


def run_local(g, blk0, count, cols, x, dy, b, c, cumt, cumr, bounds, off, carry):
    tok = x.shape[0]
    hg = cols // P_SIZE
    piece = pl.BlockSpec((BLOCK, cols), lambda i: (blk0 + i, g))
    thin = pl.BlockSpec((BLOCK, LANES), lambda i: (blk0 + i, 0))
    in_specs = [SMEM(), SMEM(), piece, piece, thin, thin, thin, pl.BlockSpec((hg, BLOCK), lambda i: (g, blk0 + i))]
    operands = [bounds, off, x, dy, b, c, cumt, cumr]
    aliases = {}
    if carry is not None:
        in_specs += [ANY()] * 4
        aliases = {8 + i: i for i in range(4)}
        operands += list(carry)
    return pl.pallas_call(
        functools.partial(local_kernel, blk0, g * hg, bounds.shape[0], carry is not None),
        grid=(count,),
        out_shape=[
            jax.ShapeDtypeStruct((tok, cols), F32),
            jax.ShapeDtypeStruct((tok, N), F32),
            jax.ShapeDtypeStruct((tok, N), F32),
            jax.ShapeDtypeStruct((hg, tok), F32),
        ],
        in_specs=in_specs,
        out_specs=[
            pl.BlockSpec((BLOCK, cols), lambda i: (blk0 + i, 0)),
            thin,
            thin,
            pl.BlockSpec((hg, BLOCK), lambda i: (0, blk0 + i)),
        ],
        scratch_shapes=[
            pltpu.VMEM((BLOCK, BLOCK), F32),
            pltpu.VMEM((BLOCK, BLOCK), F32),
            pltpu.VMEM((hg, BLOCK), F32),
        ],
        input_output_aliases=aliases,
        compiler_params=params(),
        cost_estimate=pl.CostEstimate(
            flops=16 * BLOCK * BLOCK * cols * count, bytes_accessed=BLOCK * cols * 8 * count, transcendentals=0
        ),
        name="local",
    )(*operands)


def run_enter(g, cols, order, count, x, dy, b, c, fsb, teb, edge, keep, got, st, co, dxl, wb, wc, rows, grads, whole):
    tok, wide = x.shape
    nb = tok // BLOCK
    hg = cols // P_SIZE

    def spec(shape, place):
        return pl.BlockSpec(shape, lambda i, o: place(lax.rem(o[0] + i, nb)))

    piece = spec((BLOCK, cols), lambda k: (k, g))
    thin = spec((BLOCK, LANES), lambda k: (k, 0))
    packed = pl.BlockSpec((2, BLOCK, N), lambda i, o: (0, i, 0))
    state = spec((1, N, cols), lambda k: (k, 0, 0))
    in_specs = [piece, piece, thin, thin, thin, thin]
    in_specs.append(spec((16, LANES), lambda k: (0, 0)))
    in_specs += [spec((2 * N, cols // 2), lambda k: (0, 0))] * 2
    in_specs += [state, state, spec((BLOCK, cols), lambda k: (k, 0)), thin, thin]
    in_specs.append(spec((hg, BLOCK), lambda k: (0, k)))
    operands = [order, x, dy, b, c, fsb, teb, edge, keep, got, st, co, dxl, wb, wc, rows]
    aliases = {}
    if grads is not None:
        aliases = {16: 1}
        in_specs.append(packed)
        operands.append(grads)
    if whole is not None:
        aliases[len(operands)] = 0
        aliases[len(operands) + 1] = 2
        in_specs += [ANY(), ANY()]
        operands += list(whole)
    dx, grads, gl = pl.pallas_call(
        functools.partial(enter_kernel, nb, g * hg, grads is not None, whole is not None),
        grid_spec=pltpu.PrefetchScalarGridSpec(
            num_scalar_prefetch=1,
            grid=(count,),
            in_specs=in_specs,
            out_specs=[piece, packed, spec((hg, BLOCK), lambda k: (g, k))],
            scratch_shapes=[
                pltpu.VMEM((2 * LANES, cols), BF16),
                pltpu.VMEM((cols, LANES), BF16),
                pltpu.VMEM((16, cols), F32),
            ],
        ),
        out_shape=[
            jax.ShapeDtypeStruct((tok, wide), BF16),
            jax.ShapeDtypeStruct((2, count * BLOCK, N), F32),
            jax.ShapeDtypeStruct((wide // P_SIZE, tok), F32),
        ],
        input_output_aliases=aliases,
        compiler_params=params(),
        cost_estimate=pl.CostEstimate(
            flops=20 * BLOCK * count * N * cols, bytes_accessed=BLOCK * count * cols * 12, transcendentals=0
        ),
        name="enter",
    )(*operands)
    return grads, (dx, gl)


def pick_by(index, options):
    out = options[0]
    for i in range(1, len(options)):
        out = jnp.where(index == i, options[i], out)
    return out


def parts_of(pay):
    return pay[:N], pay[N : 2 * N], pay[2 * N : 2 * N + 1]


def scan_over_seq(mine, theirs, n_seq, me, in_two):
    mid_n = n_seq // (2 * OUTER)
    core = me % 2
    mid = (me // 2) % mid_n
    half = mine.shape[1]
    w = half // mid_n

    def at(i):
        return i // (2 * mid_n), (i // 2) % mid_n, i % 2

    def index(o, m, c):
        return (o * mid_n + m) * 2 + c

    every = range(n_seq)
    swap = [(i, i ^ 1) for i in every]

    def mid_perm(s):
        return [(i, index(at(i)[0], (at(i)[1] + s) % mid_n, at(i)[2])) for i in every]

    def outer_perm(s):
        return [(i, (i + s * 2 * mid_n) % n_seq) for i in every]

    (got,) = yield [(theirs, swap)]
    f0, b0, d0 = parts_of(jnp.where(core == 0, mine, got))
    f1, b1, d1 = parts_of(jnp.where(core == 0, got, mine))
    chip = jnp.concatenate([d1 * f0 + f1, b0 + d0 * b1, jnp.broadcast_to(d0 * d1, (8, half))], axis=0)

    slices = [chip[:, q * w : (q + 1) * w] for q in range(mid_n)]
    own = pick_by(mid, slices)
    pieces = []
    for s in range(1, mid_n):
        v = pick_by((mid + s) % mid_n, slices)
        cuts = [v[:N], v[N:]] if in_two else [v]
        pieces += [(cut, mid_perm(s)) for cut in cuts]
    got = yield pieces
    step = 2 if in_two else 1
    recv = [own] + [jnp.concatenate(got[i : i + step], axis=0) for i in range(0, len(got), step)]
    chips = [parts_of(pick_by((mid - q) % mid_n, recv)) for q in range(mid_n)]
    pf, pb, pd = chips[0]
    for f, b, d in chips[1:]:
        pf, pb, pd = d * pf + f, pb + pd * b, pd * d
    outer = me // (2 * mid_n)
    pd8 = jnp.broadcast_to(pd, (16, w))
    sends = []
    for s in range(1, OUTER):
        up = outer + s < OUTER
        sends.append((jnp.concatenate([jnp.where(up, pf, pb), pd8], axis=0), outer_perm(s)))
    got = yield sends

    def fold(arrived, reach):
        acc = jnp.zeros((N, w), F32)
        for s in range(OUTER - 1, 0, -1):
            v = arrived[s - 1]
            acc = jnp.where(s <= reach, v[:N] + v[N : N + 1] * acc, 0.0)
        return acc

    ef = fold(got, outer)
    eb = fold(got[::-1], OUTER - 1 - outer)
    enter_f = []
    for f, b, d in chips:
        enter_f.append(ef)
        ef = d * ef + f
    enter_b = []
    for f, b, d in chips[::-1]:
        enter_b.append(eb)
        eb = b + d * eb
    enters = [jnp.concatenate(v, axis=0) for v in zip(enter_f, enter_b[::-1])]
    got = yield [(pick_by((mid + s) % mid_n, enters), mid_perm(s)) for s in range(1, mid_n)]
    back = [pick_by(mid, enters)] + got
    chip_e = jnp.concatenate([pick_by((mid - q) % mid_n, back) for q in range(mid_n)], axis=1)
    cf, cb = chip_e[:N], chip_e[N:]
    first = jnp.concatenate([cf, b1 + d1 * cb], axis=0)
    second = jnp.concatenate([f0 + d0 * cf, cb], axis=0)
    keep = jnp.where(core == 0, first, second)
    (got,) = yield [(jnp.where(core == 0, second, first), swap)]
    yield keep, got


def on_device(n_seq, n_head, x, dy, b, c, lf, bounds):
    tok, wide = x.shape
    hl = lf.shape[0]
    nb = tok // BLOCK
    me = lax.axis_index("seq")
    off = (me * tok).astype(jnp.int32).reshape(1)
    groups = 2 if wide // 2 >= n_seq // OUTER * LANES else 1
    cols = wide // groups
    core = (me % 2).astype(jnp.int32)
    sums = [None] * groups
    scans = [None] * groups
    enters = [None] * groups
    sends = [None] * groups
    done = [0] * groups
    parts = [None] * groups
    made = (bounds, off, lf)
    out = None

    def summarise(g):
        nonlocal made
        halves, sums[g], made = run_summary(g, cols, core, x, dy, b, c, made)
        scans[g] = scan_over_seq(*halves, n_seq, me, g == 1)
        sends[g] = next(scans[g])

    def local(g, count):
        parts[g] = run_local(g, done[g], count, cols, x, dy, b, c, made[0], made[1], bounds, off, parts[g])
        done[g] += count

    me_head = lax.axis_index("head").astype(jnp.int32)
    in_phases = nb % n_head == 0
    per = nb // n_head if in_phases else 0
    others = lax.rem(me_head + 1, n_head) * per
    phases = ((jnp.stack([others, core]), nb - per), (jnp.stack([me_head * per, core]), per))
    grads = [None, None]

    def enter(g, phase):
        nonlocal out
        order, count = phases[phase]
        args = (x, dy, b, c, *made[2:], *enters[g], *sums[g], *parts[g])
        grads[phase], out = run_enter(g, cols, order, count, *args, grads[phase], out)

    flying = [None] * groups

    def fly(g):
        flying[g] = [lax.ppermute(v, "seq", p) for v, p in sends[g]]

    def land(*landing):
        nonlocal made, parts, out, grads
        arrived = [flying[g] for g in landing]
        arrived, made, parts, out, grads = lax.optimization_barrier((arrived, made, parts, out, grads))
        for g, got in zip(landing, arrived):
            nxt = scans[g].send(got)
            if isinstance(nxt, list):
                sends[g] = nxt
            else:
                enters[g] = nxt

    summarise(0)
    if groups == 1:
        for blocks in (1, 1, nb - 2, 0, 0):
            fly(0)
            if blocks:
                local(0, blocks)
            land(0)
    else:
        fly(0)
        local(0, 1)
        land(0)
        fly(0)
        summarise(1)
        land(0)
        fly(0)
        fly(1)
        local(0, nb - 1)
        land(1)
        fly(1)
        local(1, 2)
        land(0, 1)
        fly(0)
        fly(1)
        local(1, nb - 2)
        land(0)
        fly(0)
        land(0)
        enter(0, 0)
        land(1)
        fly(1)
        if in_phases:
            enter(0, 1)
        land(1)
        fly(1)
        land(1)
    enter(groups - 1, 0)
    away, out = lax.optimization_barrier((grads[0], out))
    rows = tok // n_head

    def rows_for(s):
        start = (s - 1) * rows if in_phases else lax.rem(me_head + s, n_head) * rows
        return lax.dynamic_slice_in_dim(away, start, rows, 1)

    arrived = []
    for s in range(1, n_head):
        perm = [(i, (i + s) % n_head) for i in range(n_head)]
        arrived.append(lax.ppermute(rows_for(s), "head", perm))
    if in_phases:
        enter(groups - 1, 1)
    dx, gl = out
    total = ((grads[1] if in_phases else rows_for(0)) + sum(arrived)).astype(BF16)
    return dx, total[0], total[1], gl


def solution(mesh):
    return jax.shard_map(
        functools.partial(on_device, mesh.shape["seq"], mesh.shape["head"]),
        mesh=mesh,
        in_specs=(
            P("seq", "head"),
            P("seq", "head"),
            P("seq", None),
            P("seq", None),
            P("head", "seq"),
            P(),
        ),
        out_specs=(
            P("seq", "head"),
            P(("seq", "head"), None),
            P(("seq", "head"), None),
            P("head", "seq"),
        ),
        check_vma=False,
    )
```

```python
import functools

import jax
import jax.numpy as jnp
from jax import lax
from jax.experimental import pallas as pl
from jax.experimental.pallas import tpu as pltpu
from jax.sharding import PartitionSpec as P

P_SIZE = 64
N = 128
BLOCK = 256
TILE = 256
HPT = TILE // P_SIZE
LANES = 128
OUTER = 4
LOG2E = 1.4426950408889634
F32 = jnp.float32
BF16 = jnp.bfloat16

NN = (((1,), (0,)), ((), ()))
NT = (((1,), (1,)), ((), ()))
TN = (((0,), (0,)), ((), ()))


def mm(a, b, dims=NN):
    return lax.dot_general(a, b, dims, preferred_element_type=F32)


def split2(v):
    hi = v.astype(BF16)
    return hi, (v - hi.astype(F32)).astype(BF16)


def split3(v):
    hi = v.astype(BF16)
    rest = v - hi.astype(F32)
    mid = rest.astype(BF16)
    return hi, mid, (rest - mid.astype(F32)).astype(BF16)


def iota2(shape, dim):
    return lax.broadcasted_iota(jnp.int32, shape, dim)


def ones_where(cond):
    return jnp.where(cond, 1.0, 0.0).astype(BF16)


def expander(first_head, cols):
    r = iota2((2 * LANES, cols), 0) & (LANES - 1)
    c = iota2((2 * LANES, cols), 1) >> 6
    return ones_where(r == c + first_head)


def collector(cols):
    c = iota2((cols, LANES), 0) >> 6
    h = iota2((cols, LANES), 1)
    return ones_where(h == c)


def side_by_side(v):
    return jnp.concatenate(split2(v), axis=1)


def stack2(v):
    return jnp.concatenate(split2(v), axis=0)


def collect(v, onehot):
    hi, lo = split2(v)
    return mm(hi, onehot) + mm(lo, onehot)


def contract_states(scaled, stacked):
    hi, lo = split2(scaled)
    both = mm(hi, stacked, NT)
    return both[:, :N] + both[:, N:] + mm(lo, stacked[:N], NT)


def tri(cond_of):
    return ones_where(cond_of(iota2((BLOCK, BLOCK), 0), iota2((BLOCK, BLOCK), 1)))


def prepare(nb, nbounds, bounds, off, lf_ref, cumt_ref, cumr_ref, fsb_ref, teb_ref, edge_ref):
    hl = lf_ref.shape[0]
    tok = nb * BLOCK
    lower = tri(lambda t, s: s <= t)
    upper = tri(lambda s, t: s <= t)
    local = [bounds[k] - off[0] for k in range(nbounds)]

    def first_from(start):
        out = tok
        for v in local:
            out = jnp.minimum(out, jnp.where(v >= start, v, tok))
        return out

    def last_before(end):
        out = -1
        for v in local:
            out = jnp.maximum(out, jnp.where(v < end, v, -1))
        return out

    t_loc = iota2((BLOCK, LANES), 0)
    lasts = []
    for b in range(nb):
        rows = slice(b * BLOCK, (b + 1) * BLOCK)
        lf_pad = jnp.concatenate([lf_ref[:, rows], jnp.zeros((LANES - hl, BLOCK), F32)], axis=0)
        parts = split3(lf_pad)
        cumt = sum(mm(lower, p, NT) for p in parts)
        cumr = sum(mm(p, upper) for p in parts)
        cumt_ref[rows, :] = cumt * LOG2E
        cumr_ref[:, rows] = cumr[:hl] * LOG2E
        last = cumt[BLOCK - 1 : BLOCK]
        lasts.append(last)
        t = t_loc + b * BLOCK
        fsb_ref[rows, :] = jnp.where(t >= first_from(b * BLOCK), 0.0, jnp.exp(cumt))
        teb_ref[rows, :] = jnp.where(
            t < last_before((b + 1) * BLOCK), 0.0, jnp.exp(jnp.minimum(last - cumt, 0.0))
        )
    zero = jnp.zeros((1, LANES), F32)
    first = first_from(0)
    final = last_before(tok)
    for b in range(8):
        if b < nb:
            into = jnp.exp(sum(lasts[:b], zero))
            outof = jnp.exp(sum(lasts[b + 1 :], zero))
            edge_ref[b : b + 1, :] = jnp.where(first >= b * BLOCK, into, 0.0)
            edge_ref[8 + b : 9 + b, :] = jnp.where(final < (b + 1) * BLOCK, outof, 0.0)
        else:
            edge_ref[b : b + 1, :] = zero
            edge_ref[8 + b : 9 + b, :] = zero


def summary_kernel(nb, head0, nbounds, preparing, base, *refs):
    x_ref, dy_ref, b_ref, c_ref = refs[:4]
    i = pl.program_id(0)
    tiles = pl.num_programs(0)
    if preparing:
        bounds, off, lf_ref = refs[4:7]
        mine_ref, theirs_ref, st_ref, co_ref, *made = refs[7:]
        fsb_ref, teb_ref = made[2:4]

        @pl.when(i == 0)
        def _():
            prepare(nb, nbounds, bounds, off, lf_ref, *made)

    else:
        fsb_ref, teb_ref, mine_ref, theirs_ref, st_ref, co_ref = refs[4:]
    oh2 = expander(head0 + lax.rem(base[0] + i, tiles) * HPT, TILE)
    state = jnp.zeros((N, TILE), F32)
    costate = jnp.zeros((N, TILE), F32)
    whole = jnp.ones((1, TILE), F32)
    tots = [
        mm(side_by_side(fsb_ref[(b + 1) * BLOCK - 8 : (b + 1) * BLOCK, :]), oh2)[7:8] for b in range(nb)
    ]
    for b in range(nb):
        rows = slice(b * BLOCK, (b + 1) * BLOCK)
        st_ref[b] = state
        te = mm(side_by_side(teb_ref[rows, :]), oh2)
        hi, lo = split2(x_ref[rows, :].astype(F32) * te)
        bb = b_ref[rows, :]
        state = tots[b] * state + (mm(bb, hi, TN) + mm(bb, lo, TN))
        r = nb - 1 - b
        rows = slice(r * BLOCK, (r + 1) * BLOCK)
        co_ref[r] = costate
        fs = mm(side_by_side(fsb_ref[rows, :]), oh2)
        hi, lo = split2(dy_ref[rows, :].astype(F32) * fs)
        cc = c_ref[rows, :]
        costate = tots[r] * costate + (mm(cc, hi, TN) + mm(cc, lo, TN))
        whole = whole * tots[b]

    def put(ref):
        ref[0:N] = state
        ref[N : 2 * N] = costate
        ref[2 * N : 2 * N + 8] = jnp.broadcast_to(whole, (8, TILE))

    @pl.when(i < tiles // 2)
    def _():
        put(theirs_ref)

    @pl.when(i >= tiles // 2)
    def _():
        put(mine_ref)


def local_kernel(blk0, head0, nbounds, chained, *refs):
    refs = list(refs)
    bounds, off, x_ref, dy_ref, b_ref, c_ref, cumt_ref, cumr_ref = refs[:8]
    dx_ref, wb_ref, wc_ref, rows_ref, gt, wt, rows_s = refs[12:] if chained else refs[8:]
    start = off[0] + (blk0 + pl.program_id(0)) * BLOCK
    half = BLOCK // 2
    pairs = x_ref.shape[1] // LANES

    def segments(shape, dim):
        pos = iota2(shape, dim) + start
        seg = jnp.zeros(shape, jnp.int32)
        for k in range(nbounds):
            seg = seg + jnp.where(pos >= bounds[k], 1, 0)
        return seg

    ok = (segments((BLOCK, 1), 0) == segments((1, BLOCK), 1)) & (
        iota2((BLOCK, BLOCK), 0) <= iota2((BLOCK, BLOCK), 1)
    )
    bb = b_ref[...]
    cc = c_ref[...]
    gt[...] = jnp.where(ok, mm(bb, cc, NT), 0.0)
    wt[...] = jnp.zeros_like(wt)
    low_lane = iota2((BLOCK, LANES), 1) < P_SIZE
    for p in range(pairs):
        lanes = slice(p * LANES, (p + 1) * LANES)
        xp = x_ref[:, lanes]
        dyp = dy_ref[:, lanes]
        none = jnp.zeros_like(xp)
        picked = jnp.concatenate([jnp.where(low_lane, xp, none), jnp.where(low_lane, none, xp)], axis=0)
        prod = mm(picked, dyp, NT)
        tops = []
        bots = []
        acc = None
        for q in range(2):
            k = 2 * p + q
            pq = prod[q * BLOCK : (q + 1) * BLOCK]
            cr = cumr_ref[k : k + 1, :]
            cb = jnp.broadcast_to(cumt_ref[:, head0 + k : head0 + k + 1], (BLOCK, half))
            d00 = jnp.exp2(jnp.minimum(cr[:, :half] - cb[:half], 0.0))
            d01 = jnp.exp2(cr[:, half:] - cb[:half])
            d11 = jnp.exp2(jnp.minimum(cr[:, half:] - cb[half:], 0.0))
            a00 = pq[:half, :half] * d00
            a01 = pq[:half, half:] * d01
            a11 = pq[half:, half:] * d11
            acc = (a00, a01, a11) if q == 0 else (acc[0] + a00, acc[1] + a01, acc[2] + a11)
            g00 = gt[:half, :half]
            g01 = gt[:half, half:]
            g11 = gt[half:, half:]
            rows_s[k : k + 1, :half] = jnp.sum(a00 * g00, axis=0, keepdims=True)
            rows_s[k : k + 1, half:] = jnp.sum(a01 * g01 + a11 * g11, axis=0, keepdims=True)
            h00, l00 = split2(d00 * g00)
            h01, l01 = split2(d01 * g01)
            h11, l11 = split2(d11 * g11)
            tops.append(jnp.concatenate([h00, h01, l00, l01], axis=1))
            bots.append(jnp.concatenate([h11, l11], axis=1))
        wt[:half, :half] += acc[0]
        wt[:half, half:] += acc[1]
        wt[half:, half:] += acc[2]
        dyh = dyp[half:]
        top = mm(jnp.concatenate(tops, axis=0), jnp.concatenate([dyp, dyp], axis=0))
        bot = mm(jnp.concatenate(bots, axis=0), jnp.concatenate([dyh, dyh], axis=0))
        low = low_lane[:half]
        dx_ref[:half, lanes] = jnp.where(low, top[:half], top[half:])
        dx_ref[half:, lanes] = jnp.where(low, bot[:half], bot[half:])
    hi, lo = split2(jnp.where(ok, wt[...], 0.0))
    wb_ref[...] = mm(hi, cc) + mm(lo, cc)
    wc_ref[...] = mm(hi, bb, TN) + mm(lo, bb, TN)
    upper = tri(lambda r, a: r < a)
    rows_ref[...] = sum(mm(v, upper) for v in split3(rows_s[...]))


def enter_kernel(nb, head0, adding, aliased, *refs):
    refs = list(refs)
    order = refs[0]
    x_ref, dy_ref, b_ref, c_ref, fsb_ref, teb_ref, edge_ref, ek_ref, eg_ref, st_ref, co_ref, dxl_ref, wb, wc, rows_ref = refs[1:16]
    refs = refs[16:]
    if adding:
        prev = refs[0]
        refs = refs[1:]
    if aliased:
        refs = refs[2:]
    dx_ref, grad_ref, gl_ref, oh2, pick, edges = refs
    b = lax.rem(order[0] + pl.program_id(0), nb)
    cols = x_ref.shape[1]
    hg = gl_ref.shape[0]

    @pl.when(pl.program_id(0) == 0)
    def _():
        oh2[...] = expander(head0, cols)
        pick[...] = collector(cols)
        edges[...] = mm(side_by_side(edge_ref[...]), oh2[...])

    fcat = side_by_side(fsb_ref[...])
    tcat = side_by_side(teb_ref[...])
    bcat = jnp.concatenate([b_ref[...]] * 2, axis=1)
    ccat = jnp.concatenate([c_ref[...]] * 2, axis=1)
    gb = wb[...]
    gc = wc[...]
    if adding:
        gb = gb + prev[0]
        gc = gc + prev[1]
    col = jnp.zeros((BLOCK, LANES), F32)
    later = jnp.zeros((BLOCK, LANES), F32)
    end_row = iota2((8, TILE), 0) == 7
    for i in range(cols // TILE):
        side, begin = divmod(i * TILE, cols // 2)
        lanes = pl.ds(pl.multiple_of(lax.rem(order[1] + side, 2) * (cols // 2) + begin, TILE), TILE)
        te = mm(tcat, oh2[:, lanes])
        fs = mm(fcat, oh2[:, lanes])
        e = (eg_ref if side else ek_ref)[:, begin : begin + TILE]
        state = st_ref[0, :, lanes] + edges[pl.ds(b, 1), lanes] * e[:N]
        costate = co_ref[0, :, lanes] + edges[pl.ds(8 + b, 1), lanes] * e[N:]
        joined = fs[BLOCK - 1 :] * jnp.sum(state * costate, axis=0, keepdims=True)
        sst = stack2(state)
        gst = stack2(costate)
        x = x_ref[:, lanes].astype(F32)
        xs = x * te
        dys = dy_ref[:, lanes].astype(F32) * fs
        dx = dxl_ref[:, lanes] + te * mm(bcat, gst)
        dx_ref[:, lanes] = dx.astype(BF16)
        read = dys * mm(ccat, sst)
        read = jnp.concatenate([read[:-8], read[-8:] + jnp.where(end_row, joined, 0.0)], axis=0)
        col = col + collect(x * dx, pick[lanes, :])
        later = later + collect(read, pick[lanes, :])
        gc = gc + contract_states(dys, sst)
        gb = gb + contract_states(xs, gst)
    grad_ref[0] = gb
    grad_ref[1] = gc
    before = tri(lambda a, r: r < a)
    onward = tri(lambda a, r: r >= a)
    glt = sum(mm(before, v) for v in split3(col)) + sum(mm(onward, v) for v in split3(later))
    gl_ref[...] = jnp.transpose(glt)[:hg] - rows_ref[...]


def params(mib=58):
    return pltpu.CompilerParams(vmem_limit_bytes=mib * 1024 * 1024)


SMEM = functools.partial(pl.BlockSpec, memory_space=pltpu.SMEM)
ANY = functools.partial(pl.BlockSpec, memory_space=pl.ANY)


def run_summary(g, cols, core, x, dy, b, c, made):
    tok = x.shape[0]
    nb = tok // BLOCK
    tiles = cols // TILE
    t0 = g * tiles
    base = ((1 - core) * (tiles // 2)).astype(jnp.int32).reshape(1)

    def spec(shape, place):
        return pl.BlockSpec(shape, lambda i, o: place(i, lax.rem(o[0] + i, tiles)))

    tall = spec((tok, TILE), lambda i, j: (0, t0 + j))
    full = spec((tok, LANES), lambda i, j: (0, 0))
    blocks = spec((nb, N, TILE), lambda i, j: (0, 0, j))
    in_specs = [tall, tall, full, full]
    operands = [base, x, dy, b, c]
    half = (2 * N + 8, cols // 2)
    shapes = [half, half, (nb, N, cols), (nb, N, cols)]
    out_specs = [
        spec((2 * N + 8, TILE), lambda i, j: (0, jnp.maximum(i - tiles // 2, 0))),
        spec((2 * N + 8, TILE), lambda i, j: (0, jnp.minimum(i, tiles // 2 - 1))),
        blocks,
        blocks,
    ]
    preparing = len(made) == 3
    nbounds = 0
    if preparing:
        bounds, off, lf = made
        nbounds = bounds.shape[0]
        hl = lf.shape[0]
        in_specs += [SMEM(), SMEM(), spec((hl, tok), lambda i, j: (0, 0))]
        extra = [(tok, LANES), (hl, tok), (tok, LANES), (tok, LANES), (16, LANES)]
        shapes += extra
        out_specs += [spec(v, lambda i, j: (0, 0)) for v in extra]
        operands += [bounds, off, lf]
    else:
        in_specs += [full, full]
        operands += [made[2], made[3]]
    out = pl.pallas_call(
        functools.partial(summary_kernel, nb, g * cols // P_SIZE, nbounds, preparing),
        grid_spec=pltpu.PrefetchScalarGridSpec(
            num_scalar_prefetch=1, grid=(tiles,), in_specs=in_specs, out_specs=out_specs
        ),
        out_shape=[jax.ShapeDtypeStruct(v, F32) for v in shapes],
        compiler_params=params(),
        cost_estimate=pl.CostEstimate(flops=8 * tok * N * cols, bytes_accessed=tok * cols * 12, transcendentals=0),
        name="summary",
    )(*operands)
    return out[:2], out[2:4], out[4:] if preparing else made


def run_local(g, blk0, count, cols, x, dy, b, c, cumt, cumr, bounds, off, carry):
    tok = x.shape[0]
    hg = cols // P_SIZE
    piece = pl.BlockSpec((BLOCK, cols), lambda i: (blk0 + i, g))
    thin = pl.BlockSpec((BLOCK, LANES), lambda i: (blk0 + i, 0))
    in_specs = [SMEM(), SMEM(), piece, piece, thin, thin, thin, pl.BlockSpec((hg, BLOCK), lambda i: (g, blk0 + i))]
    operands = [bounds, off, x, dy, b, c, cumt, cumr]
    aliases = {}
    if carry is not None:
        in_specs += [ANY()] * 4
        aliases = {8 + i: i for i in range(4)}
        operands += list(carry)
    return pl.pallas_call(
        functools.partial(local_kernel, blk0, g * hg, bounds.shape[0], carry is not None),
        grid=(count,),
        out_shape=[
            jax.ShapeDtypeStruct((tok, cols), F32),
            jax.ShapeDtypeStruct((tok, N), F32),
            jax.ShapeDtypeStruct((tok, N), F32),
            jax.ShapeDtypeStruct((hg, tok), F32),
        ],
        in_specs=in_specs,
        out_specs=[
            pl.BlockSpec((BLOCK, cols), lambda i: (blk0 + i, 0)),
            thin,
            thin,
            pl.BlockSpec((hg, BLOCK), lambda i: (0, blk0 + i)),
        ],
        scratch_shapes=[
            pltpu.VMEM((BLOCK, BLOCK), F32),
            pltpu.VMEM((BLOCK, BLOCK), F32),
            pltpu.VMEM((hg, BLOCK), F32),
        ],
        input_output_aliases=aliases,
        compiler_params=params(),
        cost_estimate=pl.CostEstimate(
            flops=16 * BLOCK * BLOCK * cols * count, bytes_accessed=BLOCK * cols * 8 * count, transcendentals=0
        ),
        name="local",
    )(*operands)


def run_enter(g, cols, order, count, x, dy, b, c, fsb, teb, edge, keep, got, st, co, dxl, wb, wc, rows, grads, whole):
    tok, wide = x.shape
    nb = tok // BLOCK
    hg = cols // P_SIZE

    def spec(shape, place):
        return pl.BlockSpec(shape, lambda i, o: place(lax.rem(o[0] + i, nb)))

    piece = spec((BLOCK, cols), lambda k: (k, g))
    thin = spec((BLOCK, LANES), lambda k: (k, 0))
    packed = pl.BlockSpec((2, BLOCK, N), lambda i, o: (0, i, 0))
    state = spec((1, N, cols), lambda k: (k, 0, 0))
    in_specs = [piece, piece, thin, thin, thin, thin]
    in_specs.append(spec((16, LANES), lambda k: (0, 0)))
    in_specs += [spec((2 * N, cols // 2), lambda k: (0, 0))] * 2
    in_specs += [state, state, spec((BLOCK, cols), lambda k: (k, 0)), thin, thin]
    in_specs.append(spec((hg, BLOCK), lambda k: (0, k)))
    operands = [order, x, dy, b, c, fsb, teb, edge, keep, got, st, co, dxl, wb, wc, rows]
    aliases = {}
    if grads is not None:
        aliases = {16: 1}
        in_specs.append(packed)
        operands.append(grads)
    if whole is not None:
        aliases[len(operands)] = 0
        aliases[len(operands) + 1] = 2
        in_specs += [ANY(), ANY()]
        operands += list(whole)
    dx, grads, gl = pl.pallas_call(
        functools.partial(enter_kernel, nb, g * hg, grads is not None, whole is not None),
        grid_spec=pltpu.PrefetchScalarGridSpec(
            num_scalar_prefetch=1,
            grid=(count,),
            in_specs=in_specs,
            out_specs=[piece, packed, spec((hg, BLOCK), lambda k: (g, k))],
            scratch_shapes=[
                pltpu.VMEM((2 * LANES, cols), BF16),
                pltpu.VMEM((cols, LANES), BF16),
                pltpu.VMEM((16, cols), F32),
            ],
        ),
        out_shape=[
            jax.ShapeDtypeStruct((tok, wide), BF16),
            jax.ShapeDtypeStruct((2, count * BLOCK, N), F32),
            jax.ShapeDtypeStruct((wide // P_SIZE, tok), F32),
        ],
        input_output_aliases=aliases,
        compiler_params=params(46),
        cost_estimate=pl.CostEstimate(
            flops=20 * BLOCK * count * N * cols, bytes_accessed=BLOCK * count * cols * 12, transcendentals=0
        ),
        name="enter",
    )(*operands)
    return grads, (dx, gl)


def pick_by(index, options):
    out = options[0]
    for i in range(1, len(options)):
        out = jnp.where(index == i, options[i], out)
    return out


def parts_of(pay):
    return pay[:N], pay[N : 2 * N], pay[2 * N : 2 * N + 1]


def scan_over_seq(mine, theirs, n_seq, me, in_two):
    mid_n = n_seq // (2 * OUTER)
    core = me % 2
    mid = (me // 2) % mid_n
    half = mine.shape[1]
    w = half // mid_n

    def at(i):
        return i // (2 * mid_n), (i // 2) % mid_n, i % 2

    def index(o, m, c):
        return (o * mid_n + m) * 2 + c

    every = range(n_seq)
    swap = [(i, i ^ 1) for i in every]

    def mid_perm(s):
        return [(i, index(at(i)[0], (at(i)[1] + s) % mid_n, at(i)[2])) for i in every]

    def outer_perm(s):
        return [(i, (i + s * 2 * mid_n) % n_seq) for i in every]

    (got,) = yield [(theirs, swap)]
    f0, b0, d0 = parts_of(jnp.where(core == 0, mine, got))
    f1, b1, d1 = parts_of(jnp.where(core == 0, got, mine))
    chip = jnp.concatenate([d1 * f0 + f1, b0 + d0 * b1, jnp.broadcast_to(d0 * d1, (8, half))], axis=0)

    slices = [chip[:, q * w : (q + 1) * w] for q in range(mid_n)]
    own = pick_by(mid, slices)
    pieces = []
    for s in range(1, mid_n):
        v = pick_by((mid + s) % mid_n, slices)
        cuts = [v[:N], v[N:]] if in_two else [v]
        pieces += [(cut, mid_perm(s)) for cut in cuts]
    got = yield pieces
    step = 2 if in_two else 1
    recv = [own] + [jnp.concatenate(got[i : i + step], axis=0) for i in range(0, len(got), step)]
    chips = [parts_of(pick_by((mid - q) % mid_n, recv)) for q in range(mid_n)]
    pf, pb, pd = chips[0]
    for f, b, d in chips[1:]:
        pf, pb, pd = d * pf + f, pb + pd * b, pd * d
    outer = me // (2 * mid_n)
    pd8 = jnp.broadcast_to(pd, (16, w))
    sends = []
    for s in range(1, OUTER):
        up = outer + s < OUTER
        sends.append((jnp.concatenate([jnp.where(up, pf, pb), pd8], axis=0), outer_perm(s)))
    got = yield sends

    def fold(arrived, reach):
        acc = jnp.zeros((N, w), F32)
        for s in range(OUTER - 1, 0, -1):
            v = arrived[s - 1]
            acc = jnp.where(s <= reach, v[:N] + v[N : N + 1] * acc, 0.0)
        return acc

    ef = fold(got, outer)
    eb = fold(got[::-1], OUTER - 1 - outer)
    enter_f = []
    for f, b, d in chips:
        enter_f.append(ef)
        ef = d * ef + f
    enter_b = []
    for f, b, d in chips[::-1]:
        enter_b.append(eb)
        eb = b + d * eb
    enters = [jnp.concatenate(v, axis=0) for v in zip(enter_f, enter_b[::-1])]
    got = yield [(pick_by((mid + s) % mid_n, enters), mid_perm(s)) for s in range(1, mid_n)]
    back = [pick_by(mid, enters)] + got
    chip_e = jnp.concatenate([pick_by((mid - q) % mid_n, back) for q in range(mid_n)], axis=1)
    cf, cb = chip_e[:N], chip_e[N:]
    first = jnp.concatenate([cf, b1 + d1 * cb], axis=0)
    second = jnp.concatenate([f0 + d0 * cf, cb], axis=0)
    keep = jnp.where(core == 0, first, second)
    (got,) = yield [(jnp.where(core == 0, second, first), swap)]
    yield keep, got


def on_device(n_seq, n_head, x, dy, b, c, lf, bounds):
    tok, wide = x.shape
    hl = lf.shape[0]
    nb = tok // BLOCK
    me = lax.axis_index("seq")
    off = (me * tok).astype(jnp.int32).reshape(1)
    groups = 2 if wide // 2 >= n_seq // OUTER * LANES else 1
    cols = wide // groups
    core = (me % 2).astype(jnp.int32)
    sums = [None] * groups
    scans = [None] * groups
    enters = [None] * groups
    sends = [None] * groups
    done = [0] * groups
    parts = [None] * groups
    made = (bounds, off, lf)
    out = None

    def summarise(g):
        nonlocal made
        halves, sums[g], made = run_summary(g, cols, core, x, dy, b, c, made)
        scans[g] = scan_over_seq(*halves, n_seq, me, g == 1)
        sends[g] = next(scans[g])

    def local(g, count):
        parts[g] = run_local(g, done[g], count, cols, x, dy, b, c, made[0], made[1], bounds, off, parts[g])
        done[g] += count

    me_head = lax.axis_index("head").astype(jnp.int32)
    in_phases = nb % n_head == 0
    per = nb // n_head if in_phases else 0
    others = lax.rem(me_head + 1, n_head) * per
    phases = ((jnp.stack([others, core]), nb - per), (jnp.stack([me_head * per, core]), per))
    grads = [None, None]

    def enter(g, phase):
        nonlocal out
        order, count = phases[phase]
        args = (x, dy, b, c, *made[2:], *enters[g], *sums[g], *parts[g])
        grads[phase], out = run_enter(g, cols, order, count, *args, grads[phase], out)

    flying = [None] * groups

    def fly(g):
        flying[g] = [lax.ppermute(v, "seq", p) for v, p in sends[g]]

    def land(*landing):
        nonlocal made, parts, out, grads
        arrived = [flying[g] for g in landing]
        arrived, made, parts, out, grads = lax.optimization_barrier((arrived, made, parts, out, grads))
        for g, got in zip(landing, arrived):
            nxt = scans[g].send(got)
            if isinstance(nxt, list):
                sends[g] = nxt
            else:
                enters[g] = nxt

    summarise(0)
    if groups == 1:
        for blocks in (1, 1, nb - 2, 0, 0):
            fly(0)
            if blocks:
                local(0, blocks)
            land(0)
    else:
        fly(0)
        local(0, 1)
        land(0)
        fly(0)
        summarise(1)
        land(0)
        fly(0)
        fly(1)
        local(0, nb - 1)
        land(1)
        fly(1)
        local(1, 2)
        land(0, 1)
        fly(0)
        fly(1)
        local(1, nb - 2)
        land(0)
        fly(0)
        land(0)
        enter(0, 0)
        land(1)
        fly(1)
        if in_phases:
            enter(0, 1)
        land(1)
        fly(1)
        land(1)
    enter(groups - 1, 0)
    away, out = lax.optimization_barrier((grads[0], out))
    rows = tok // n_head

    def rows_for(s):
        start = (s - 1) * rows if in_phases else lax.rem(me_head + s, n_head) * rows
        return lax.dynamic_slice_in_dim(away, start, rows, 1)

    arrived = []
    for s in range(1, n_head):
        perm = [(i, (i + s) % n_head) for i in range(n_head)]
        arrived.append(lax.ppermute(rows_for(s), "head", perm))
    if in_phases:
        enter(groups - 1, 1)
    dx, gl = out
    total = ((grads[1] if in_phases else rows_for(0)) + sum(arrived)).astype(BF16)
    return dx, total[0], total[1], gl


def solution(mesh):
    return jax.shard_map(
        functools.partial(on_device, mesh.shape["seq"], mesh.shape["head"]),
        mesh=mesh,
        in_specs=(
            P("seq", "head"),
            P("seq", "head"),
            P("seq", None),
            P("seq", None),
            P("head", "seq"),
            P(),
        ),
        out_specs=(
            P("seq", "head"),
            P(("seq", "head"), None),
            P(("seq", "head"), None),
            P("head", "seq"),
        ),
        check_vma=False,
    )
```
